512 devices in a mesh: dp: 16 (over y, z_hi), row: 8 (over z_lo, core), col: 4 (over x).
Axes of the slice: x: 4, y: 4, z: 16 (z_hi: 4, z_lo: 4; z = z_hi * 4 + z_lo), core: 2. Of those that a mesh axis runs over, the one named last changes fastest.
Arguments:
- tokens: bfloat16 [16, 128, 64, 768], P('dp', 'row', 'col'), may hold values from -32 to 32
- w_qkv: bfloat16 [768, 1152], replicated, may hold values from -1 to 1
- grad_out: bfloat16 [16, 128, 64, 384], P('dp', 'row', 'col'), may hold values from -1.5 to 1.5
Outputs:
- attended: bfloat16 [16, 128, 64, 384], P('dp', 'row', 'col')
- grad_tokens: bfloat16 [16, 128, 64, 768], P('dp', 'row', 'col')
- grad_w: float32 [768, 1152], P(('row', 'col'), 'dp')
The draws below stay inside these ranges and needn't reach their ends.
All inputs are finite; a program needn't handle non-finite values.
Results may differ from the reference program's by a relative error of at most 0.025.
Values may be sent and summed in bfloat16 or wider, within the bound.
A program may use at most 64 MiB of HBM per device.

```python
import jax
import jax.numpy as jnp
from jax import lax

D = 768
HEADS = 6
HEAD = 64
TILE = 8
IMAGES = 16
IMG_ROWS = 128
IMG_COLS = 64


def draw_tokens(key, part):
    shape = (IMAGES, IMG_ROWS, IMG_COLS, D)
    key_base = jax.random.fold_in(key, 0)
    base = jnp.clip(jax.random.normal(key_base, shape, jnp.float32), -4.0, 4.0)
    return base.astype(jnp.bfloat16)


def draw_w_qkv(key, part):
    width = HEADS * HEAD
    key_main = jax.random.fold_in(key, 0)
    scale = D ** (-0.5)
    main = jnp.clip(jax.random.normal(key_main, (D, 3 * width), jnp.float32), -4.0, 4.0) * scale
    return main.astype(jnp.bfloat16)


def block_scale(rng, shape, cuts, smallest, top_value):
    def one(dim, parts):
        steps = jax.random.uniform(jax.random.fold_in(jax.random.fold_in(rng, 6), dim), (parts,), jnp.float32, smallest / len(cuts), top_value / len(cuts))
        return jnp.repeat(jnp.exp(steps), shape[dim] // parts).reshape((-1,) + (1,) * (len(shape) - dim - 1))

    level = one(*cuts[0])
    for cut in cuts[1:]:
        level = level * one(*cut)
    return level


def scatter_about(rng, extent, scale, most, cuts=(), kind=jnp.bfloat16):
    gain = block_scale(rng, extent, cuts, -0.22, 0.18) if cuts else 1.0
    drawn = jax.random.normal(rng, extent, jnp.float32) * scale * gain
    return jnp.minimum(jnp.maximum(drawn, -most), most).astype(kind)


def setup_inputs(seed: int = 0) -> dict:
    streams_of = jax.random.split(jax.random.key(seed), 4)
    return {
        "tokens": draw_tokens(jax.random.fold_in(streams_of[3], 71), 0),
        "w_qkv": draw_w_qkv(jax.random.fold_in(streams_of[3], 71), 0),
        "grad_out": scatter_about(streams_of[2], (IMAGES, IMG_ROWS, IMG_COLS, HEADS * HEAD), 0.25, 1.5, ((0, 16), (1, 8), (2, 4))),
    }


def tiles_of(image):
    row_len, col_len, feats = image.shape
    tiled = image.reshape(row_len // TILE, TILE, col_len // TILE, TILE, feats).transpose(0, 2, 1, 3, 4)
    return tiled.reshape((row_len // TILE) * (col_len // TILE), TILE * TILE, feats)


def image_of(tiled, row_len, col_len):
    feats = tiled.shape[-1]
    image = tiled.reshape(row_len // TILE, col_len // TILE, TILE, TILE, feats).transpose(0, 2, 1, 3, 4)
    return image.reshape(row_len, col_len, feats)


def beside_all(padded, row_len, col_len):
    pieces = [tiles_of(padded[down_off * TILE:down_off * TILE + row_len, side_off * TILE:side_off * TILE + col_len]) for down_off in range(3) for side_off in range(3)]
    return jnp.concatenate(pieces, axis=1)


def spread_back(near, row_len, col_len):
    feats = near.shape[-1]
    blocks = near.reshape(near.shape[0], 9, TILE * TILE, feats)
    total = jnp.zeros((row_len + 2 * TILE, col_len + 2 * TILE, feats), jnp.float32)
    for down_off in range(3):
        for side_off in range(3):
            piece = image_of(blocks[:, 3 * down_off + side_off], row_len, col_len)
            total = total + jnp.pad(piece, ((down_off * TILE, (2 - down_off) * TILE), (side_off * TILE, (2 - side_off) * TILE), (0, 0)))
    return total


def one_image(image, cotangent, w_qkv):
    row_len, col_len = IMG_ROWS, IMG_COLS
    width = HEADS * HEAD
    scale = HEAD ** -0.5
    qkv = jnp.dot(image.reshape(-1, D), w_qkv, preferred_element_type=jnp.float32)
    qkv = lax.optimization_barrier(qkv.astype(jnp.bfloat16)).reshape(row_len, col_len, 3 * width)
    rim = ((TILE, TILE), (TILE, TILE), (0, 0))
    key_near = beside_all(jnp.pad(qkv[..., width:], rim), row_len, col_len)
    valid = beside_all(jnp.pad(jnp.ones((row_len, col_len, 1), jnp.float32), rim), row_len, col_len)[..., 0] > 0.5
    query_t = tiles_of(qkv[..., :width])
    count = query_t.shape[0]
    queries = query_t.reshape(count, TILE * TILE, HEADS, HEAD).astype(jnp.float32)
    keys = key_near[..., :width].reshape(count, -1, HEADS, HEAD).astype(jnp.float32)
    values = key_near[..., width:].reshape(count, -1, HEADS, HEAD).astype(jnp.float32)
    cot_t = tiles_of(cotangent).reshape(count, TILE * TILE, HEADS, HEAD).astype(jnp.float32)
    scores = jnp.einsum('tqhe,tkhe->thqk', queries, keys) * scale
    scores = jnp.where(valid[:, None, None, :], scores, -1e30)
    peak = jnp.max(scores, axis=-1, keepdims=True)
    expd = jnp.exp(scores - peak)
    probs = expd / jnp.sum(expd, axis=-1, keepdims=True)
    probs_b = lax.optimization_barrier(probs.astype(jnp.bfloat16)).astype(jnp.float32)
    output = jnp.einsum('thqk,tkhe->tqhe', probs_b, values).astype(jnp.bfloat16)
    dprobs = jnp.einsum('tqhe,tkhe->thqk', cot_t, values)
    delta = jnp.sum(probs * dprobs, axis=-1, keepdims=True)
    dscores = lax.optimization_barrier((probs * (dprobs - delta) * scale).astype(jnp.bfloat16)).astype(jnp.float32)
    grad_q = jnp.einsum('thqk,tkhe->tqhe', dscores, keys)
    grad_k = jnp.einsum('thqk,tqhe->tkhe', dscores, queries)
    grad_v = jnp.einsum('thqk,tqhe->tkhe', probs_b, cot_t)
    near_grads = jnp.concatenate([grad_k.reshape(count, -1, width), grad_v.reshape(count, -1, width)], axis=-1)
    kv_grads = spread_back(near_grads, row_len, col_len)[TILE:TILE + row_len, TILE:TILE + col_len]
    q_grads = image_of(grad_q.reshape(count, -1, width), row_len, col_len)
    dqkv = jnp.concatenate([q_grads, kv_grads], axis=-1).astype(jnp.bfloat16).reshape(-1, 3 * width)
    grad_x = jnp.dot(dqkv, w_qkv.T, preferred_element_type=jnp.float32).astype(jnp.bfloat16).reshape(row_len, col_len, D)
    grad_term = jnp.dot(image.reshape(-1, D).T, dqkv, preferred_element_type=jnp.float32)
    attended = image_of(output.reshape(count, -1, width), row_len, col_len)
    return attended, grad_x, grad_term


def reference(tokens, w_qkv, grad_out):
    def advance(total, pair):
        attended, grad_x, grad_term = one_image(pair[0], pair[1], w_qkv)
        return total + grad_term, (attended, grad_x)

    start = jnp.zeros((D, 3 * HEADS * HEAD), jnp.float32)
    total, (attended, grad_tokens) = lax.scan(advance, start, (tokens, grad_out))
    return attended, grad_tokens, total / IMAGES
```

```python
import functools

import jax
import jax.numpy as jnp
from jax import lax
from jax.experimental import pallas as pl
from jax.experimental.pallas import tpu as pltpu
from jax.sharding import PartitionSpec as P

D = 768
HEADS = 6
HEAD = 64
TILE = 8
F = HEADS * HEAD
KV = 2 * F
SIDE = 16
BF = jnp.bfloat16
F32 = jnp.float32
MESH = pl.DeviceIdType.MESH
BIG = -1e30
VLIM = 60 * 1024 * 1024


def dot(a, b, ca=1, cb=0):
    return lax.dot_general(a, b, (((ca,), (cb,)), ((), ())), preferred_element_type=F32)


def remote(src, dst, ssem, rsem, dev):
    return pltpu.make_async_remote_copy(
        src_ref=src, dst_ref=dst, send_sem=ssem, recv_sem=rsem, device_id=dev, device_id_type=MESH
    )


def position():
    dp, row, col = lax.axis_index("dp"), lax.axis_index("row"), lax.axis_index("col")
    return dp, row, col


def halo_kernel(nrow, ncol, tok, reg, ssem, rsem):
    dp, row, col = position()
    has_l, has_r = col > 0, col < ncol - 1
    has_u, has_d = row > 0, row < nrow - 1
    left, right = (dp, row, jnp.maximum(col - 1, 0)), (dp, row, jnp.minimum(col + 1, ncol - 1))
    up, down = (dp, jnp.maximum(row - 1, 0), col), (dp, jnp.minimum(row + 1, nrow - 1), col)

    bar = pltpu.get_barrier_semaphore()
    for cond, dev in ((has_l, left), (has_r, right), (has_u, up), (has_d, down)):

        @pl.when(cond)
        def _(dev=dev):
            pl.semaphore_signal(bar, inc=1, device_id=dev, device_id_type=MESH)

    i32 = jnp.int32
    pl.semaphore_wait(
        bar, has_l.astype(i32) + has_r.astype(i32) + has_u.astype(i32) + has_d.astype(i32)
    )

    T = TILE
    plan = [
        (has_l, has_r, tok.at[0, :, 0:T], reg.at[3, T : 3 * T], left),
        (has_r, has_l, tok.at[0, :, T : 2 * T], reg.at[0, T : 3 * T], right),
    ]
    for j in range(2):
        cols = slice(T * j, T * j + T)
        plan.append((has_u, has_d, tok.at[0, 0:T, cols], reg.at[1 + j, 3 * T : 4 * T], up))
        plan.append((has_d, has_u, tok.at[0, T : 2 * T, cols], reg.at[1 + j, 0:T], down))
    for side, has in ((0, has_l), (3, has_r)):
        plan.append(
            (has & has_u, has & has_d, reg.at[side, T : 2 * T], reg.at[side, 3 * T : 4 * T], up)
        )
        plan.append((has & has_d, has & has_u, reg.at[side, 2 * T : 3 * T], reg.at[side, 0:T], down))

    def copy(n):
        _, _, src, dst, dev = plan[n]
        return remote(src, dst, ssem.at[n], rsem.at[n], dev)

    def start(n):
        @pl.when(plan[n][0])
        def _():
            copy(n).start()

    def arrived(n):
        @pl.when(plan[n][1])
        def _():
            copy(n).wait_recv()

    for n in range(6):
        start(n)
    arrived(1)
    start(6)
    start(7)
    arrived(0)
    start(8)
    start(9)
    for n in range(2, 10):
        arrived(n)
    for n in range(10):

        @pl.when(plan[n][0])
        def _(n=n):
            copy(n).wait_send()


def main_kernel(nrow, ncol, ndp, tok, w, cot, reg, att_o, gx_o, gw_o, s):
    dp, row, col = position()
    zl, core = row // 2, row % 2
    y, zh = dp // 4, dp % 4
    z = zh * 4 + zl
    x = col
    sib_row = row + 1 - 2 * core
    has_l, has_r = col > 0, col < ncol - 1
    has_u, has_d = row > 0, row < nrow - 1
    left, right = (dp, row, jnp.maximum(col - 1, 0)), (dp, row, jnp.minimum(col + 1, ncol - 1))
    up, down = (dp, jnp.maximum(row - 1, 0), col), (dp, jnp.minimum(row + 1, nrow - 1), col)
    sibling = (dp, sib_row, col)
    x_p, x_m = (dp, row, (col + 1) % 4), (dp, row, (col + 3) % 4)
    y_p, y_m = (((y + 1) % 4) * 4 + zh, row, col), (((y + 3) % 4) * 4 + zh, row, col)

    def z_peer(d):
        other = (z + d) % 16
        return other, (y * 4 + other // 4, (other % 4) * 2 + core, col)

    T = TILE
    loads = [
        pltpu.make_async_copy(reg.at[0], s.reg.at[0], s.lsem.at[0]),
        pltpu.make_async_copy(reg.at[3], s.reg.at[3], s.lsem.at[1]),
        pltpu.make_async_copy(reg.at[1:3, 0:T], s.reg.at[1:3, 0:T], s.lsem.at[2]),
        pltpu.make_async_copy(reg.at[1:3, 3 * T : 4 * T], s.reg.at[1:3, 3 * T : 4 * T], s.lsem.at[3]),
        pltpu.make_async_copy(tok.at[0, :, 0:T], s.reg.at[1, T : 3 * T], s.lsem.at[4]),
        pltpu.make_async_copy(tok.at[0, :, T : 2 * T], s.reg.at[2, T : 3 * T], s.lsem.at[5]),
        pltpu.make_async_copy(w, s.w, s.lsem.at[6]),
        pltpu.make_async_copy(cot, s.cot, s.lsem.at[7]),
    ]
    for c in loads:
        c.start()

    bar = pltpu.get_barrier_semaphore()

    def greet(dev):
        pl.semaphore_signal(bar, inc=1, device_id=dev, device_id_type=MESH)

    for d in range(1, 16):
        greet(z_peer(d)[1])
    for dev in (x_p, x_m, y_p, y_m, sibling):
        greet(dev)
    other_row = row - 1 + 2 * core
    has_other = (other_row >= 0) & (other_row < nrow)

    @pl.when(has_other)
    def _():
        greet((dp, jnp.clip(other_row, 0, nrow - 1), col))

    def tile_ok(ti, tj):
        gr, gc = row * 2 + ti - 1, col * 2 + tj - 1
        return (gr >= 0) & (gr < 2 * nrow) & (gc >= 0) & (gc < 2 * ncol)

    for c in loads:
        c.wait()

    def tile_tokens(tj, carry):
        for ti in range(4):
            piece = s.reg[tj, T * ti : T * ti + T].astype(F32).reshape(64, D)
            piece = jnp.where(tile_ok(ti, tj), piece, 0.0)
            s.xf[64 * ti : 64 * ti + 64, :] = piece
        full = s.xf[...]
        base = pl.multiple_of(tj * 256, 256)
        s.xr[pl.ds(base, 256), :] = full.astype(BF)
        turned = full.T.reshape(4, 2, 4, 24, 256).transpose(1, 2, 0, 3, 4).reshape(D, 256)
        s.xt[:, pl.ds(base, 256)] = turned.astype(BF)
        kv = dot(s.xr[pl.ds(base, 256), :], s.w[:, F : 3 * F]).astype(BF)
        s.kv[pl.ds(base, 256), :] = kv
        s.kvt[:, pl.ds(base, 256)] = kv.astype(F32).T.astype(BF)
        s.acc[pl.ds(base, 256), :] = jnp.zeros((256, KV), F32)
        return carry

    lax.fori_loop(0, 4, tile_tokens, 0)
    for j in range(2):
        own = s.xr[(1 + j) * 256 + 64 : (1 + j) * 256 + 192, :]
        s.xto[:, 128 * j : 128 * j + 128] = s.xt[:, (1 + j) * 256 + 64 : (1 + j) * 256 + 192]
        q = dot(own, s.w[:, :F]).astype(BF).astype(F32) * (HEAD**-0.5)
        s.q[128 * j : 128 * j + 128, :] = q.astype(BF)
        c = s.cot[0, :, T * j : T * j + T, :].astype(F32).reshape(128, F)
        s.c[128 * j : 128 * j + 128, :] = c.astype(BF)

    def one_tile(t, carry):
        j, i = t // 2, t % 2
        qrow = pl.multiple_of(j * 128 + i * 64, 64)
        for g0, W in ((0, 256), (256, 128)):
            nh = W // HEAD
            rows_i = lax.broadcasted_iota(jnp.int32, (W, W), 0) // HEAD
            cols_i = lax.broadcasted_iota(jnp.int32, (W, W), 1) // HEAD
            mask = rows_i == cols_i
            lanes = slice(g0, g0 + W)
            vlanes = slice(F + g0, F + g0 + W)

            def block_diag(part):
                part = part.astype(F32)
                return jnp.where(mask, jnp.concatenate([part] * nh, axis=0), 0.0).astype(BF)

            qbd = block_diag(s.q[pl.ds(qrow, 64), lanes])
            cbd = block_diag(s.c[pl.ds(qrow, 64), lanes])
            peak = None
            for a in range(3):
                base = pl.multiple_of((j + a) * 256 + 64 * i, 64)
                sc = dot(s.kv[pl.ds(base, 192), lanes], qbd, 1, 1)
                parts = []
                for b in range(3):
                    bias = jnp.where(tile_ok(i + b, j + a), 0.0, BIG)
                    parts.append(sc[64 * b : 64 * b + 64] + bias)
                sc = jnp.concatenate(parts, axis=0)
                s.sc[192 * a : 192 * a + 192, :W] = sc
                top = jnp.max(sc, axis=0, keepdims=True)
                peak = top if peak is None else jnp.maximum(peak, top)
                s.dp[192 * a : 192 * a + 192, :W] = dot(s.kv[pl.ds(base, 192), vlanes], cbd, 1, 1)
            total = 0.0
            for a in range(3):
                rows = slice(192 * a, 192 * a + 192)
                e = jnp.exp(s.sc[rows, :W] - peak)
                s.sc[rows, :W] = e
                total = total + jnp.sum(e, axis=0, keepdims=True)
            inv = 1.0 / total
            delta = 0.0
            for a in range(3):
                rows = slice(192 * a, 192 * a + 192)
                delta = delta + jnp.sum(s.sc[rows, :W] * inv * s.dp[rows, :W], axis=0, keepdims=True)
            for a in range(3):
                rows = slice(192 * a, 192 * a + 192)
                base = pl.multiple_of((j + a) * 256 + 64 * i, 64)
                p = s.sc[rows, :W] * inv
                pb = p.astype(BF)
                db = (p * (s.dp[rows, :W] - delta)).astype(BF)
                to = pl.multiple_of(a * 256 + 64 * i, 64)
                zero = pl.multiple_of(a * 256 + 192 * (1 - i), 64)
                s.pt[pl.ds(to, 192), :W] = pb
                s.ds[pl.ds(to, 192), :W] = db
                s.pt[pl.ds(zero, 64), :W] = jnp.zeros((64, W), BF)
                s.ds[pl.ds(zero, 64), :W] = jnp.zeros((64, W), BF)
                s.acc[pl.ds(base, 192), lanes] += dot(db, qbd)
                s.acc[pl.ds(base, 192), vlanes] += dot(pb, cbd)
            wide = pl.ds(pl.multiple_of(256 * j, 256), 768)

            def fold(turned):
                kept = jnp.where(mask, turned, 0.0).T
                out = kept[0:64]
                for h in range(1, nh):
                    out = out + kept[64 * h : 64 * h + 64]
                return out

            o = fold(dot(s.kvt[vlanes, wide], s.pt[:, :W]))
            s.att[pl.ds(8 * i, 8), pl.ds(8 * j, 8), lanes] = o.reshape(8, 8, W)
            dq = fold(dot(s.kvt[lanes, wide], s.ds[:, :W])) * (HEAD**-0.5)
            s.dq[pl.ds(qrow, 64), lanes] = dq
        return carry

    lax.fori_loop(0, 4, one_tile, 0)
    att_o[0] = s.att[...].astype(BF)

    zeros96 = jnp.zeros((256, 96), F32)

    def pack(tj, carry):
        rows = pl.ds(pl.multiple_of(tj * 256, 256), 256)
        k = s.acc[rows, :F]
        v = s.acc[rows, F:]
        s.dkv[rows, :F] = k.astype(BF)
        s.dkv[rows, F:] = v.astype(BF)
        s.pad[rows, 0:384] = jnp.concatenate([zeros96, k[:, 0:192], zeros96], axis=1).astype(BF)
        s.pad[rows, 384:768] = jnp.concatenate([k[:, 192:384], v[:, 0:96], zeros96], axis=1).astype(BF)
        s.pad[rows, 768:1152] = jnp.concatenate([v[:, 96:384], zeros96], axis=1).astype(BF)
        return carry

    lax.fori_loop(0, 4, pack, 0)
    dqv = s.dq[...]
    s.qpad[:, 0:384] = jnp.concatenate([dqv[:, :288], zeros96], axis=1).astype(BF)
    s.qpad[:, 384:768] = jnp.concatenate([dqv[:, 288:], zeros96, zeros96, zeros96], axis=1).astype(BF)

    pl.semaphore_wait(bar, 20 + has_other.astype(jnp.int32))

    vert = []
    for n, tj in enumerate((0, 3, 1, 2)):
        side = has_l if tj == 0 else has_r if tj == 3 else None
        for m, (has, back, ti, dev) in enumerate(((has_u, has_d, 0, up), (has_d, has_u, 3, down))):
            at = tj * 256 + ti * 64
            cp = remote(
                s.dkv.at[at : at + 64], s.vr.at[m, tj], s.vs.at[2 * n + m], s.vw.at[2 * n + m], dev
            )
            snd, rcv = (has, back) if side is None else (has & side, back & side)
            vert.append((snd, rcv, cp))
            pl.when(snd)(cp.start)

    def grads(half):
        at = pl.ds(pl.multiple_of(half * 384, 384), 384)
        xo, xa = s.xto[at, :], s.xt[at, :]
        return xo, xa

    def grad_half(half, put):
        xo, xa = grads(half)
        put(slice(0, 384), dot(xo, s.qpad[:, 0:384]))
        put(slice(384, 768), dot(xo, s.qpad[:, 384:768]) + dot(xa, s.pad[:, 0:384]))
        put(slice(768, 1152), dot(xa, s.pad[:, 384:768]))
        put(slice(1152, 1536), dot(xa, s.pad[:, 768:1152]))

    def put_send(lanes, value):
        s.gs[:, lanes] = value.astype(BF)

    def put_own(lanes, value):
        s.s1[:, lanes] = value

    grad_half(1 - core, put_send)
    pair = remote(s.gs, s.gr, s.ps.at[0], s.pw.at[0], sibling)
    pair.start()
    grad_half(core, put_own)
    pair.wait()
    s.s1[...] = s.s1[...] + s.gr[...].astype(F32)
    s.s1b[...] = s.s1[...].astype(BF)

    class Ring:
        def __init__(self, m, plus, minus, half_b, half_f, buf, sems, at):
            self.m, self.half_f, self.buf = m, half_f, buf
            o, p, q = (m + 2) % 4, (m + 1) % 4, (m + 3) % 4
            self.p, self.q = p, q
            ss, rs = sems

            def cp(src, dst, n, dev):
                return remote(src, dst, ss.at[at + n], rs.at[at + n], dev)

            self.first = [
                cp(half_b(o, 0), buf.at[0], 0, plus),
                cp(half_b(o, 1), buf.at[1], 1, minus),
                cp(half_b(p, 1), buf.at[3], 2, plus),
                cp(half_b(q, 0), buf.at[4], 3, minus),
            ]
            self.second = [
                cp(buf.at[6], buf.at[2], 4, plus),
                cp(buf.at[7], buf.at[5], 5, minus),
            ]

        def start(self):
            for c in self.first:
                c.start()

        def relay(self):
            buf = self.buf
            self.first[0].wait_recv()
            buf[6] = (self.half_f(self.p, 0) + buf[0].astype(F32)).astype(BF)
            self.second[0].start()
            self.first[1].wait_recv()
            buf[7] = (self.half_f(self.q, 1) + buf[1].astype(F32)).astype(BF)
            self.second[1].start()

        def finish(self):
            buf, m = self.buf, self.m
            self.first[2].wait_recv()
            self.first[3].wait_recv()
            self.second[0].wait_recv()
            self.second[1].wait_recv()
            lo = self.half_f(m, 0) + buf[2].astype(F32) + buf[4].astype(F32)
            hi = self.half_f(m, 1) + buf[3].astype(F32) + buf[5].astype(F32)
            return lo, hi

        def sent(self):
            for c in self.first + self.second:
                c.wait_send()

    def al(v, n):
        return pl.multiple_of(v, n)

    ax = Ring(
        x, x_p, x_m,
        lambda k, h: s.s1b.at[pl.ds(al(k * 96, 96), 96), 768 * h : 768 * h + 768],
        lambda k, h: s.s1[pl.ds(al(k * 96, 96), 96), 768 * h : 768 * h + 768],
        s.bx, (s.as_, s.aw), 0,
    )
    ay = Ring(
        y, y_p, y_m,
        lambda k, h: s.s1b.at[192 * h : 192 * h + 192, pl.ds(al(k * 384, 384), 384)],
        lambda k, h: s.s1[192 * h : 192 * h + 192, pl.ds(al(k * 384, 384), 384)],
        s.by, (s.as_, s.aw), 6,
    )

    @pl.when(core == 0)
    def _():
        ax.start()

    @pl.when(core == 1)
    def _():
        ay.start()

    for n in range(4):
        snd, rcv, cp = vert[n]
        pl.when(rcv)(cp.wait_recv)
    horiz = []
    for m, (has, back, tj, dev) in enumerate(((has_l, has_r, 0, left), (has_r, has_l, 3, right))):
        base = tj * 256 + 64
        cp = remote(s.hs.at[m], s.hr.at[m], s.hsem.at[m], s.hw.at[m], dev)
        horiz.append((has, back, cp))

        @pl.when(has)
        def _(m=m, base=base, tj=tj, cp=cp):
            upper = s.acc[base : base + 64, :]
            lower = s.acc[base + 64 : base + 128, :]
            upper = upper + jnp.where(has_u, s.vr[1, tj].astype(F32), 0.0)
            lower = lower + jnp.where(has_d, s.vr[0, tj].astype(F32), 0.0)
            s.hs[m, 0:64] = upper.astype(BF)
            s.hs[m, 64:128] = lower.astype(BF)
            cp.start()

    @pl.when(core == 0)
    def _():
        ax.relay()

    @pl.when(core == 1)
    def _():
        ay.relay()

    @pl.when(core == 0)
    def _():
        lo, hi = ax.finish()
        s.s2x[:, 0:768] = lo
        s.s2x[:, 768:1536] = hi
        s.s2xb[:, 0:768] = lo.astype(BF)
        s.s2xb[:, 768:1536] = hi.astype(BF)

    @pl.when(core == 1)
    def _():
        lo, hi = ay.finish()
        s.s2y[0:192] = lo
        s.s2y[192:384] = hi
        s.s2yb[0:192] = lo.astype(BF)
        s.s2yb[192:384] = hi.astype(BF)

    by = Ring(
        y, y_p, y_m,
        lambda k, h: s.s2xb.at[48 * h : 48 * h + 48, pl.ds(al(k * 384, 384), 384)],
        lambda k, h: s.s2x[48 * h : 48 * h + 48, pl.ds(al(k * 384, 384), 384)],
        s.b2, (s.bs, s.bw), 0,
    )
    bx = Ring(
        x, x_p, x_m,
        lambda k, h: s.s2yb.at[pl.ds(al(k * 96 + 48 * h, 48), 48), :],
        lambda k, h: s.s2y[pl.ds(al(k * 96 + 48 * h, 48), 48), :],
        s.b2, (s.bs, s.bw), 0,
    )

    def second(ring):
        ring.start()
        ring.relay()
        lo, hi = ring.finish()
        s.s3[0:48] = lo
        s.s3[48:96] = hi

    @pl.when(core == 0)
    def _():
        second(by)

    @pl.when(core == 1)
    def _():
        second(bx)

    s3 = s.s3[...]
    for h in range(4):
        lanes = (s3 if h == 0 else pltpu.roll(s3, 384 - 72 * h, 1))[:, :128]
        for l in range(4):
            s.zs[4 * h + l] = lanes[24 * l : 24 * l + 24].astype(BF)
    zcopies = {}
    for d in (8, 7, 9, 6, 10, 5, 11, 4, 12, 3, 13, 2, 14, 1, 15):
        other, dev = z_peer(d)
        zcopies[d] = remote(s.zs.at[other], s.zr.at[d - 1], s.zsem.at[d - 1], s.zw.at[d - 1], dev)
        zcopies[d].start()

    for n in range(4, 8):
        snd, rcv, cp = vert[n]
        pl.when(rcv)(cp.wait_recv)
    for has, back, cp in horiz:
        pl.when(back)(cp.wait_recv)
    for j in range(2):
        base = (1 + j) * 256 + 64
        own = s.acc[base : base + 128, :]
        upper = own[0:64] + jnp.where(has_u, s.vr[1, 1 + j].astype(F32), 0.0)
        lower = own[64:128] + jnp.where(has_d, s.vr[0, 1 + j].astype(F32), 0.0)
        own = jnp.concatenate([upper, lower], axis=0)
        has, m = (has_l, 1) if j == 0 else (has_r, 0)
        own = own + jnp.where(has, s.hr[m].astype(F32), 0.0)
        gx = dot(s.dq[128 * j : 128 * j + 128, :].astype(BF), s.w[:, :F], 1, 1)
        gx = gx + dot(own.astype(BF), s.w[:, F:], 1, 1)
        s.gx[:, T * j : T * j + T, :] = gx.reshape(SIDE, T, D)
    gx_o[0] = s.gx[...].astype(BF)

    total = s.zs[z].astype(F32)
    for d in range(1, 16):
        zcopies[d].wait_recv()
        total = total + s.zr[d - 1].astype(F32)
    gw_o[...] = total[:, :72] * (1.0 / ndp)

    for snd, rcv, cp in vert:
        pl.when(snd)(cp.wait_send)
    for has, back, cp in horiz:
        pl.when(has)(cp.wait_send)

    @pl.when(core == 0)
    def _():
        ax.sent()
        by.sent()

    @pl.when(core == 1)
    def _():
        ay.sent()
        bx.sent()

    for d in range(1, 16):
        zcopies[d].wait_send()


class Scratch:
    pass


V = pltpu.VMEM
DMA = pltpu.SemaphoreType.DMA
SCRATCH = dict(
    reg=V((4, 32, 8, D), BF),
    w=V((D, 3 * F), BF),
    cot=V((1, SIDE, SIDE, F), BF),
    xf=V((256, D), F32),
    xr=V((1024, D), BF),
    xt=V((D, 1024), BF),
    xto=V((D, 256), BF),
    kv=V((1024, KV), BF),
    kvt=V((KV, 1024), BF),
    q=V((256, F), BF),
    c=V((256, F), BF),
    acc=V((1024, KV), F32),
    dq=V((256, F), F32),
    att=V((SIDE, SIDE, F), F32),
    sc=V((576, 256), F32),
    dp=V((576, 256), F32),
    pt=V((768, 256), BF),
    ds=V((768, 256), BF),
    dkv=V((1024, KV), BF),
    pad=V((1024, 1152), BF),
    qpad=V((256, 768), BF),
    gx=V((SIDE, SIDE, D), F32),
    gs=V((384, 1536), BF),
    gr=V((384, 1536), BF),
    s1=V((384, 1536), F32),
    s1b=V((384, 1536), BF),
    bx=V((8, 96, 768), BF),
    by=V((8, 192, 384), BF),
    s2x=V((96, 1536), F32),
    s2xb=V((96, 1536), BF),
    s2y=V((384, 384), F32),
    s2yb=V((384, 384), BF),
    b2=V((8, 48, 384), BF),
    s3=V((96, 384), F32),
    zs=V((16, 24, 128), BF),
    zr=V((15, 24, 128), BF),
    vr=V((2, 4, 64, KV), BF),
    hs=V((2, 128, KV), BF),
    hr=V((2, 128, KV), BF),
    lsem=DMA((8,)),
    vs=DMA((8,)),
    vw=DMA((8,)),
    ps=DMA((1,)),
    pw=DMA((1,)),
    as_=DMA((12,)),
    aw=DMA((12,)),
    bs=DMA((6,)),
    bw=DMA((6,)),
    hsem=DMA((2,)),
    hw=DMA((2,)),
    zsem=DMA((15,)),
    zw=DMA((15,)),
)


def main_entry(nrow, ncol, ndp, *refs):
    s = Scratch()
    for name, ref in zip(SCRATCH, refs[7:]):
        setattr(s, name, ref)
    main_kernel(nrow, ncol, ndp, *refs[:7], s)


def body(nrow, ncol, ndp, tokens, w_qkv, grad_out):
    anywhere = pl.BlockSpec(memory_space=pl.ANY)
    vmem = pl.BlockSpec(memory_space=pltpu.VMEM)
    region = pl.pallas_call(
        functools.partial(halo_kernel, nrow, ncol),
        out_shape=jax.ShapeDtypeStruct((4, 32, 8, D), BF),
        in_specs=[anywhere],
        out_specs=anywhere,
        scratch_shapes=[DMA((10,)), DMA((10,))],
        compiler_params=pltpu.CompilerParams(collective_id=0, has_side_effects=True),
        name="halo",
    )(tokens)
    return pl.pallas_call(
        functools.partial(main_entry, nrow, ncol, ndp),
        out_shape=(
            jax.ShapeDtypeStruct((1, SIDE, SIDE, F), BF),
            jax.ShapeDtypeStruct((1, SIDE, SIDE, D), BF),
            jax.ShapeDtypeStruct((24, 72), F32),
        ),
        in_specs=[anywhere] * 4,
        out_specs=(vmem, vmem, vmem),
        scratch_shapes=list(SCRATCH.values()),
        compiler_params=pltpu.CompilerParams(
            collective_id=1, has_side_effects=True, vmem_limit_bytes=VLIM
        ),
        name="block",
    )(tokens, w_qkv, grad_out, region)


def solution(mesh):
    split = P("dp", "row", "col", None)
    sizes = mesh.shape
    return jax.shard_map(
        functools.partial(body, sizes["row"], sizes["col"], sizes["dp"]),
        mesh=mesh,
        in_specs=(split, P(), split),
        out_specs=(split, split, P(("row", "col"), "dp")),
        check_vma=False,
    )
```

```python
import functools

import jax
import jax.numpy as jnp
from jax import lax
from jax.experimental import pallas as pl
from jax.experimental.pallas import tpu as pltpu
from jax.sharding import PartitionSpec as P

D = 768
HEADS = 6
HEAD = 64
TILE = 8
F = HEADS * HEAD
KV = 2 * F
SIDE = 16
BF = jnp.bfloat16
F32 = jnp.float32
MESH = pl.DeviceIdType.MESH
BIG = -1e30
VLIM = 60 * 1024 * 1024


def dot(a, b, ca=1, cb=0):
    return lax.dot_general(a, b, (((ca,), (cb,)), ((), ())), preferred_element_type=F32)


def remote(src, dst, ssem, rsem, dev):
    return pltpu.make_async_remote_copy(
        src_ref=src, dst_ref=dst, send_sem=ssem, recv_sem=rsem, device_id=dev, device_id_type=MESH
    )


def position():
    dp, row, col = lax.axis_index("dp"), lax.axis_index("row"), lax.axis_index("col")
    return dp, row, col


def main_kernel(nrow, ncol, ndp, tok, w, cot, att_o, gx_o, gw_o, s):
    dp, row, col = position()
    zl, core = row // 2, row % 2
    y, zh = dp // 4, dp % 4
    z = zh * 4 + zl
    x = col
    sib_row = row + 1 - 2 * core
    has_l, has_r = col > 0, col < ncol - 1
    has_u, has_d = row > 0, row < nrow - 1
    left, right = (dp, row, jnp.maximum(col - 1, 0)), (dp, row, jnp.minimum(col + 1, ncol - 1))
    up, down = (dp, jnp.maximum(row - 1, 0), col), (dp, jnp.minimum(row + 1, nrow - 1), col)
    sibling = (dp, sib_row, col)
    x_p, x_m = (dp, row, (col + 1) % 4), (dp, row, (col + 3) % 4)
    y_p, y_m = (((y + 1) % 4) * 4 + zh, row, col), (((y + 3) % 4) * 4 + zh, row, col)

    def z_peer(d):
        other = (z + d) % 16
        return other, (y * 4 + other // 4, (other % 4) * 2 + core, col)

    T = TILE
    loads = [
        pltpu.make_async_copy(cot, s.cot, s.lsem.at[0]),
        pltpu.make_async_copy(tok.at[0, :, 0:T], s.reg.at[1, T : 3 * T], s.lsem.at[1]),
        pltpu.make_async_copy(tok.at[0, :, T : 2 * T], s.reg.at[2, T : 3 * T], s.lsem.at[2]),
        pltpu.make_async_copy(w, s.w, s.lsem.at[3]),
    ]
    for c in loads:
        c.start()

    bar = pltpu.get_barrier_semaphore()

    def greet(dev, sem=bar):
        pl.semaphore_signal(sem, inc=1, device_id=dev, device_id_type=MESH)

    for dev in (x_p, x_m, y_p, y_m, sibling, z_peer(1)[1], z_peer(15)[1]):
        greet(dev)
    other_row = row - 1 + 2 * core
    has_other = (other_row >= 0) & (other_row < nrow)

    @pl.when(has_other)
    def _():
        greet((dp, jnp.clip(other_row, 0, nrow - 1), col))

    pl.semaphore_wait(bar, 7 + has_other.astype(jnp.int32))

    plan = [
        (has_l, has_r, tok.at[0, :, 0:T], s.reg.at[3, T : 3 * T], left),
        (has_r, has_l, tok.at[0, :, T : 2 * T], s.reg.at[0, T : 3 * T], right),
    ]
    for j in range(2):
        cols = slice(T * j, T * j + T)
        plan.append((has_u, has_d, tok.at[0, 0:T, cols], s.reg.at[1 + j, 3 * T : 4 * T], up))
        plan.append((has_d, has_u, tok.at[0, T : 2 * T, cols], s.reg.at[1 + j, 0:T], down))
    for side, has in ((0, has_l), (3, has_r)):
        plan.append(
            (has & has_u, has & has_d, s.reg.at[side, T : 2 * T], s.reg.at[side, 3 * T : 4 * T], up)
        )
        plan.append(
            (has & has_d, has & has_u, s.reg.at[side, 2 * T : 3 * T], s.reg.at[side, 0:T], down)
        )

    def halo(n):
        _, _, src, dst, dev = plan[n]
        return remote(src, dst, s.hs_.at[n], s.hw_.at[n], dev)

    def start(n):
        pl.when(plan[n][0])(lambda: halo(n).start())

    def arrived(n):
        pl.when(plan[n][1])(lambda: halo(n).wait_recv())

    for n in range(6):
        start(n)

    for dev in (x_p, x_m, y_p, y_m):
        greet(dev, s.seen.at[0])
    for dev in (z_peer(1)[1], z_peer(15)[1]):
        greet(dev, s.seen.at[1])

    def tile_ok(ti, tj):
        gr, gc = row * 2 + ti - 1, col * 2 + tj - 1
        return (gr >= 0) & (gr < 2 * nrow) & (gc >= 0) & (gc < 2 * ncol)

    def tile_tokens(tj, carry):
        for ti in range(4):
            piece = s.reg[tj, T * ti : T * ti + T].astype(F32).reshape(64, D)
            piece = jnp.where(tile_ok(ti, tj), piece, 0.0)
            s.xf[64 * ti : 64 * ti + 64, :] = piece
        full = s.xf[...]
        base = pl.multiple_of(tj * 256, 256)
        s.xr[pl.ds(base, 256), :] = full.astype(BF)
        turned = full.T.reshape(4, 2, 4, 24, 256).transpose(1, 2, 0, 3, 4).reshape(D, 256)
        s.xt[:, pl.ds(base, 256)] = turned.astype(BF)
        kv = dot(s.xr[pl.ds(base, 256), :], s.w[:, F : 3 * F]).astype(BF)
        s.kv[pl.ds(base, 256), :] = kv
        s.kvt[:, pl.ds(base, 256)] = kv.astype(F32).T.astype(BF)
        s.acc[pl.ds(base, 256), :] = jnp.zeros((256, KV), F32)
        return carry

    loads[0].wait()
    loads[1].wait()
    loads[2].wait()
    for j in range(2):
        c = s.cot[0, :, T * j : T * j + T, :].astype(F32).reshape(128, F)
        s.c[128 * j : 128 * j + 128, :] = c.astype(BF)
    arrived(1)
    start(6)
    start(7)
    arrived(0)
    start(8)
    start(9)
    loads[3].wait()
    for n in range(2, 6):
        arrived(n)
    lax.fori_loop(1, 3, tile_tokens, 0)
    pl.semaphore_wait(s.seen.at[1], 2)
    greet(z_peer(2)[1], s.seen.at[2])
    greet(z_peer(14)[1], s.seen.at[2])
    for j in range(2):
        own = s.xr[(1 + j) * 256 + 64 : (1 + j) * 256 + 192, :]
        s.xto[:, 128 * j : 128 * j + 128] = s.xt[:, (1 + j) * 256 + 64 : (1 + j) * 256 + 192]
        q = dot(own, s.w[:, :F]).astype(BF).astype(F32) * (HEAD**-0.5)
        s.q[128 * j : 128 * j + 128, :] = q.astype(BF)
    for n in range(6, 10):
        arrived(n)
    lax.fori_loop(0, 2, lambda t, carry: tile_tokens(3 * t, carry), 0)
    pl.semaphore_wait(s.seen.at[2], 2)
    greet(z_peer(4)[1], s.seen.at[3])
    greet(z_peer(12)[1], s.seen.at[3])

    def one_tile(t, carry):
        j, i = t // 2, t % 2
        qrow = pl.multiple_of(j * 128 + i * 64, 64)
        for g0, W in ((0, 256), (256, 128)):
            nh = W // HEAD
            rows_i = lax.broadcasted_iota(jnp.int32, (W, W), 0) // HEAD
            cols_i = lax.broadcasted_iota(jnp.int32, (W, W), 1) // HEAD
            mask = rows_i == cols_i
            lanes = slice(g0, g0 + W)
            vlanes = slice(F + g0, F + g0 + W)

            def block_diag(part):
                part = part.astype(F32)
                return jnp.where(mask, jnp.concatenate([part] * nh, axis=0), 0.0).astype(BF)

            qbd = block_diag(s.q[pl.ds(qrow, 64), lanes])
            cbd = block_diag(s.c[pl.ds(qrow, 64), lanes])
            peak = None
            for a in range(3):
                base = pl.multiple_of((j + a) * 256 + 64 * i, 64)
                sc = dot(s.kv[pl.ds(base, 192), lanes], qbd, 1, 1)
                parts = []
                for b in range(3):
                    bias = jnp.where(tile_ok(i + b, j + a), 0.0, BIG)
                    parts.append(sc[64 * b : 64 * b + 64] + bias)
                sc = jnp.concatenate(parts, axis=0)
                s.sc[192 * a : 192 * a + 192, :W] = sc
                top = jnp.max(sc, axis=0, keepdims=True)
                peak = top if peak is None else jnp.maximum(peak, top)
                s.dp[192 * a : 192 * a + 192, :W] = dot(s.kv[pl.ds(base, 192), vlanes], cbd, 1, 1)
            total = 0.0
            for a in range(3):
                rows = slice(192 * a, 192 * a + 192)
                e = jnp.exp(s.sc[rows, :W] - peak)
                s.sc[rows, :W] = e
                total = total + jnp.sum(e, axis=0, keepdims=True)
            inv = 1.0 / total
            delta = 0.0
            for a in range(3):
                rows = slice(192 * a, 192 * a + 192)
                delta = delta + jnp.sum(s.sc[rows, :W] * inv * s.dp[rows, :W], axis=0, keepdims=True)
            for a in range(3):
                rows = slice(192 * a, 192 * a + 192)
                base = pl.multiple_of((j + a) * 256 + 64 * i, 64)
                p = s.sc[rows, :W] * inv
                pb = p.astype(BF)
                db = (p * (s.dp[rows, :W] - delta)).astype(BF)
                to = pl.multiple_of(a * 256 + 64 * i, 64)
                zero = pl.multiple_of(a * 256 + 192 * (1 - i), 64)
                s.pt[pl.ds(to, 192), :W] = pb
                s.ds[pl.ds(to, 192), :W] = db
                s.pt[pl.ds(zero, 64), :W] = jnp.zeros((64, W), BF)
                s.ds[pl.ds(zero, 64), :W] = jnp.zeros((64, W), BF)
                s.acc[pl.ds(base, 192), lanes] += dot(db, qbd)
                s.acc[pl.ds(base, 192), vlanes] += dot(pb, cbd)
            wide = pl.ds(pl.multiple_of(256 * j, 256), 768)

            def fold(turned):
                kept = jnp.where(mask, turned, 0.0).T
                out = kept[0:64]
                for h in range(1, nh):
                    out = out + kept[64 * h : 64 * h + 64]
                return out

            o = fold(dot(s.kvt[vlanes, wide], s.pt[:, :W]))
            s.att[pl.ds(8 * i, 8), pl.ds(8 * j, 8), lanes] = o.reshape(8, 8, W)
            dq = fold(dot(s.kvt[lanes, wide], s.ds[:, :W])) * (HEAD**-0.5)
            s.dq[pl.ds(qrow, 64), lanes] = dq
        return carry

    lax.fori_loop(0, 4, one_tile, 0)
    att_o[0] = s.att[...].astype(BF)

    zeros96 = jnp.zeros((256, 96), F32)

    def pack(tj, carry):
        rows = pl.ds(pl.multiple_of(tj * 256, 256), 256)
        k = s.acc[rows, :F]
        v = s.acc[rows, F:]
        s.dkv[rows, :F] = k.astype(BF)
        s.dkv[rows, F:] = v.astype(BF)
        s.pad[rows, 0:384] = jnp.concatenate([zeros96, k[:, 0:192], zeros96], axis=1).astype(BF)
        s.pad[rows, 384:768] = jnp.concatenate([k[:, 192:384], v[:, 0:96], zeros96], axis=1).astype(BF)
        s.pad[rows, 768:1152] = jnp.concatenate([v[:, 96:384], zeros96], axis=1).astype(BF)
        return carry

    lax.fori_loop(0, 4, pack, 0)
    dqv = s.dq[...]
    s.qpad[:, 0:384] = jnp.concatenate([dqv[:, :288], zeros96], axis=1).astype(BF)
    s.qpad[:, 384:768] = jnp.concatenate([dqv[:, 288:], zeros96, zeros96, zeros96], axis=1).astype(BF)

    vert = []
    for n, tj in enumerate((0, 3, 1, 2)):
        side = has_l if tj == 0 else has_r if tj == 3 else None
        for m, (has, back, ti, dev) in enumerate(((has_u, has_d, 0, up), (has_d, has_u, 3, down))):
            at = tj * 256 + ti * 64
            cp = remote(
                s.dkv.at[at : at + 64], s.vr.at[m, tj], s.vs.at[2 * n + m], s.vw.at[2 * n + m], dev
            )
            snd, rcv = (has, back) if side is None else (has & side, back & side)
            vert.append((snd, rcv, cp))
            pl.when(snd)(cp.start)

    def grads(half):
        at = pl.ds(pl.multiple_of(half * 384, 384), 384)
        xo, xa = s.xto[at, :], s.xt[at, :]
        return xo, xa

    def grad_half(half, put):
        xo, xa = grads(half)
        put(slice(0, 384), dot(xo, s.qpad[:, 0:384]))
        put(slice(384, 768), dot(xo, s.qpad[:, 384:768]) + dot(xa, s.pad[:, 0:384]))
        put(slice(768, 1152), dot(xa, s.pad[:, 384:768]))
        put(slice(1152, 1536), dot(xa, s.pad[:, 768:1152]))

    def put_send(lanes, value):
        s.gs[:, lanes] = value.astype(BF)

    def put_own(lanes, value):
        s.s1[:, lanes] = value

    grad_half(1 - core, put_send)
    pair = remote(s.gs, s.gr, s.ps.at[0], s.pw.at[0], sibling)
    pair.start()
    grad_half(core, put_own)
    pair.wait()
    s.s1[...] = s.s1[...] + s.gr[...].astype(F32)
    s.s1b[...] = s.s1[...].astype(BF)

    class Ring:
        def __init__(self, m, plus, minus, half_b, half_f, buf, sems, at):
            self.m, self.half_f, self.buf = m, half_f, buf
            o, p, q = (m + 2) % 4, (m + 1) % 4, (m + 3) % 4
            self.p, self.q = p, q
            ss, rs = sems

            def cp(src, dst, n, dev):
                return remote(src, dst, ss.at[at + n], rs.at[at + n], dev)

            self.first = [
                cp(half_b(o, 0), buf.at[0], 0, plus),
                cp(half_b(o, 1), buf.at[1], 1, minus),
                cp(half_b(p, 1), buf.at[3], 2, plus),
                cp(half_b(q, 0), buf.at[4], 3, minus),
            ]
            self.second = [
                cp(buf.at[6], buf.at[2], 4, plus),
                cp(buf.at[7], buf.at[5], 5, minus),
            ]

        def start(self):
            for c in self.first:
                c.start()

        def relay(self):
            buf = self.buf
            self.first[0].wait_recv()
            buf[6] = (self.half_f(self.p, 0) + buf[0].astype(F32)).astype(BF)
            self.second[0].start()
            self.first[1].wait_recv()
            buf[7] = (self.half_f(self.q, 1) + buf[1].astype(F32)).astype(BF)
            self.second[1].start()

        def finish(self):
            buf, m = self.buf, self.m
            self.first[2].wait_recv()
            self.first[3].wait_recv()
            self.second[0].wait_recv()
            self.second[1].wait_recv()
            lo = self.half_f(m, 0) + buf[2].astype(F32) + buf[4].astype(F32)
            hi = self.half_f(m, 1) + buf[3].astype(F32) + buf[5].astype(F32)
            return lo, hi

        def sent(self):
            for c in self.first + self.second:
                c.wait_send()

    def al(v, n):
        return pl.multiple_of(v, n)

    ax = Ring(
        x, x_p, x_m,
        lambda k, h: s.s1b.at[pl.ds(al(k * 96, 96), 96), 768 * h : 768 * h + 768],
        lambda k, h: s.s1[pl.ds(al(k * 96, 96), 96), 768 * h : 768 * h + 768],
        s.bx, (s.as_, s.aw), 0,
    )
    ay = Ring(
        y, y_p, y_m,
        lambda k, h: s.s1b.at[192 * h : 192 * h + 192, pl.ds(al(k * 384, 384), 384)],
        lambda k, h: s.s1[192 * h : 192 * h + 192, pl.ds(al(k * 384, 384), 384)],
        s.by, (s.as_, s.aw), 6,
    )

    @pl.when(core == 0)
    def _():
        ax.start()

    @pl.when(core == 1)
    def _():
        ay.start()

    @pl.when(core == 0)
    def _():
        ax.relay()

    @pl.when(core == 1)
    def _():
        ay.relay()

    for n in range(4):
        snd, rcv, cp = vert[n]
        pl.when(rcv)(cp.wait_recv)
    horiz = []
    for m, (has, back, tj, dev) in enumerate(((has_l, has_r, 0, left), (has_r, has_l, 3, right))):
        base = tj * 256 + 64
        cp = remote(s.hs.at[m], s.hr.at[m], s.hsem.at[m], s.hw.at[m], dev)
        horiz.append((has, back, cp))

        @pl.when(has)
        def _(m=m, base=base, tj=tj, cp=cp):
            upper = s.acc[base : base + 64, :]
            lower = s.acc[base + 64 : base + 128, :]
            upper = upper + jnp.where(has_u, s.vr[1, tj].astype(F32), 0.0)
            lower = lower + jnp.where(has_d, s.vr[0, tj].astype(F32), 0.0)
            s.hs[m, 0:64] = upper.astype(BF)
            s.hs[m, 64:128] = lower.astype(BF)
            cp.start()

    @pl.when(core == 0)
    def _():
        lo, hi = ax.finish()
        s.s2x[:, 0:768] = lo
        s.s2x[:, 768:1536] = hi
        s.s2xb[:, 0:768] = lo.astype(BF)
        s.s2xb[:, 768:1536] = hi.astype(BF)

    @pl.when(core == 1)
    def _():
        lo, hi = ay.finish()
        s.s2y[0:192] = lo
        s.s2y[192:384] = hi
        s.s2yb[0:192] = lo.astype(BF)
        s.s2yb[192:384] = hi.astype(BF)

    def spread(m, src, dev_of):
        copies = []
        for d in (2, 1, 3):
            k = (m + d) % 4
            cp = remote(src(k), s.b2.at[d - 1], s.bs.at[d - 1], s.bw.at[d - 1], dev_of(k))
            cp.start()
            copies.append(cp)
        return copies

    pl.semaphore_wait(s.seen.at[0], 4)

    def by():
        return spread(
            y,
            lambda k: s.s2xb.at[:, pl.ds(al(k * 384, 384), 384)],
            lambda k: (k * 4 + zh, row, col),
        )

    def bx():
        return spread(x, lambda k: s.s2yb.at[pl.ds(al(k * 96, 96), 96), :], lambda k: (dp, row, k))

    def second(copies, own):
        for cp in copies:
            cp.wait()
        s.s3[...] = own + s.b2[0].astype(F32) + s.b2[1].astype(F32) + s.b2[2].astype(F32)

    @pl.when(core == 0)
    def _():
        second(by(), s.s2x[:, pl.ds(al(y * 384, 384), 384)])

    @pl.when(core == 1)
    def _():
        second(bx(), s.s2y[pl.ds(al(x * 96, 96), 96), :])

    pl.semaphore_wait(s.seen.at[3], 2)

    s3 = s.s3[...]
    for h in range(4):
        lanes = (s3 if h == 0 else pltpu.roll(s3, 384 - 72 * h, 1))[:, :128]
        for l in range(4):
            s.zs[4 * h + l] = lanes[24 * l : 24 * l + 24].astype(BF)
    zcopies = {}
    for d in (8, 7, 9, 6, 10, 5, 11, 4, 12, 3, 13, 2, 14, 1, 15):
        other, dev = z_peer(d)
        zcopies[d] = remote(s.zs.at[other], s.zr.at[d - 1], s.zsem.at[d - 1], s.zw.at[d - 1], dev)
        zcopies[d].start()

    for n in range(4, 8):
        snd, rcv, cp = vert[n]
        pl.when(rcv)(cp.wait_recv)
    for has, back, cp in horiz:
        pl.when(back)(cp.wait_recv)
    for j in range(2):
        base = (1 + j) * 256 + 64
        own = s.acc[base : base + 128, :]
        upper = own[0:64] + jnp.where(has_u, s.vr[1, 1 + j].astype(F32), 0.0)
        lower = own[64:128] + jnp.where(has_d, s.vr[0, 1 + j].astype(F32), 0.0)
        own = jnp.concatenate([upper, lower], axis=0)
        has, m = (has_l, 1) if j == 0 else (has_r, 0)
        own = own + jnp.where(has, s.hr[m].astype(F32), 0.0)
        gx = dot(s.dq[128 * j : 128 * j + 128, :].astype(BF), s.w[:, :F], 1, 1)
        gx = gx + dot(own.astype(BF), s.w[:, F:], 1, 1)
        s.gx[:, T * j : T * j + T, :] = gx.reshape(SIDE, T, D)
    gx_o[0] = s.gx[...].astype(BF)

    total = s.zs[z].astype(F32)
    for d in range(1, 16):
        zcopies[d].wait_recv()
        total = total + s.zr[d - 1].astype(F32)
    gw_o[...] = total[:, :72] * (1.0 / ndp)

    for n in range(10):
        pl.when(plan[n][0])(lambda n=n: halo(n).wait_send())
    for snd, rcv, cp in vert:
        pl.when(snd)(cp.wait_send)
    for has, back, cp in horiz:
        pl.when(has)(cp.wait_send)

    @pl.when(core == 0)
    def _():
        ax.sent()

    @pl.when(core == 1)
    def _():
        ay.sent()

    for d in range(1, 16):
        zcopies[d].wait_send()


class Scratch:
    pass


V = pltpu.VMEM
DMA = pltpu.SemaphoreType.DMA
SCRATCH = dict(
    reg=V((4, 32, 8, D), BF),
    w=V((D, 3 * F), BF),
    cot=V((1, SIDE, SIDE, F), BF),
    xf=V((256, D), F32),
    xr=V((1024, D), BF),
    xt=V((D, 1024), BF),
    xto=V((D, 256), BF),
    kv=V((1024, KV), BF),
    kvt=V((KV, 1024), BF),
    q=V((256, F), BF),
    c=V((256, F), BF),
    acc=V((1024, KV), F32),
    dq=V((256, F), F32),
    att=V((SIDE, SIDE, F), F32),
    sc=V((576, 256), F32),
    dp=V((576, 256), F32),
    pt=V((768, 256), BF),
    ds=V((768, 256), BF),
    dkv=V((1024, KV), BF),
    pad=V((1024, 1152), BF),
    qpad=V((256, 768), BF),
    gx=V((SIDE, SIDE, D), F32),
    gs=V((384, 1536), BF),
    gr=V((384, 1536), BF),
    s1=V((384, 1536), F32),
    s1b=V((384, 1536), BF),
    bx=V((8, 96, 768), BF),
    by=V((8, 192, 384), BF),
    s2x=V((96, 1536), F32),
    s2xb=V((96, 1536), BF),
    s2y=V((384, 384), F32),
    s2yb=V((384, 384), BF),
    b2=V((3, 96, 384), BF),
    s3=V((96, 384), F32),
    zs=V((16, 24, 128), BF),
    zr=V((15, 24, 128), BF),
    vr=V((2, 4, 64, KV), BF),
    hs=V((2, 128, KV), BF),
    hr=V((2, 128, KV), BF),
    lsem=DMA((4,)),
    hs_=DMA((10,)),
    hw_=DMA((10,)),
    seen=pltpu.SemaphoreType.REGULAR((4,)),
    vs=DMA((8,)),
    vw=DMA((8,)),
    ps=DMA((1,)),
    pw=DMA((1,)),
    as_=DMA((12,)),
    aw=DMA((12,)),
    bs=DMA((3,)),
    bw=DMA((3,)),
    hsem=DMA((2,)),
    hw=DMA((2,)),
    zsem=DMA((15,)),
    zw=DMA((15,)),
)


def main_entry(nrow, ncol, ndp, *refs):
    s = Scratch()
    for name, ref in zip(SCRATCH, refs[6:]):
        setattr(s, name, ref)
    main_kernel(nrow, ncol, ndp, *refs[:6], s)


def body(nrow, ncol, ndp, tokens, w_qkv, grad_out):
    anywhere = pl.BlockSpec(memory_space=pl.ANY)
    vmem = pl.BlockSpec(memory_space=pltpu.VMEM)
    outs = (
        jax.ShapeDtypeStruct((1, SIDE, SIDE, F), BF),
        jax.ShapeDtypeStruct((1, SIDE, SIDE, D), BF),
        jax.ShapeDtypeStruct((24, 72), F32),
    )
    held = pl.pallas_call(
        functools.partial(main_entry, nrow, ncol, ndp),
        out_shape=outs,
        in_specs=[anywhere] * 3,
        out_specs=(vmem, vmem, vmem),
        scratch_shapes=list(SCRATCH.values()),
        compiler_params=pltpu.CompilerParams(
            collective_id=1, has_side_effects=True, vmem_limit_bytes=VLIM
        ),
        name="block",
    )(tokens, w_qkv, grad_out)
    return pl.pallas_call(
        hand_on,
        out_shape=outs,
        in_specs=[vmem] * 3,
        out_specs=(vmem, vmem, vmem),
        name="results",
    )(*held)


def hand_on(a, b, c, a_o, b_o, c_o):
    a_o[...] = a[...]
    b_o[...] = b[...]
    c_o[...] = c[...]


def solution(mesh):
    split = P("dp", "row", "col", None)
    sizes = mesh.shape
    return jax.shard_map(
        functools.partial(body, sizes["row"], sizes["col"], sizes["dp"]),
        mesh=mesh,
        in_specs=(split, P(), split),
        out_specs=(split, split, P(("row", "col"), "dp")),
        check_vma=False,
    )
```

```python
import functools

import jax
import jax.numpy as jnp
from jax import lax
from jax.experimental import pallas as pl
from jax.experimental.pallas import tpu as pltpu
from jax.sharding import PartitionSpec as P

D = 768
HEADS = 6
HEAD = 64
TILE = 8
F = HEADS * HEAD
KV = 2 * F
SIDE = 16
BF = jnp.bfloat16
F32 = jnp.float32
MESH = pl.DeviceIdType.MESH
BIG = -1e30
VLIM = 60 * 1024 * 1024


def dot(a, b, ca=1, cb=0):
    return lax.dot_general(a, b, (((ca,), (cb,)), ((), ())), preferred_element_type=F32)


def remote(src, dst, ssem, rsem, dev):
    return pltpu.make_async_remote_copy(
        src_ref=src, dst_ref=dst, send_sem=ssem, recv_sem=rsem, device_id=dev, device_id_type=MESH
    )


def position():
    dp, row, col = lax.axis_index("dp"), lax.axis_index("row"), lax.axis_index("col")
    return dp, row, col


def main_kernel(nrow, ncol, ndp, tok, w, cot, att_o, gx_o, gw_o, s):
    dp, row, col = position()
    zl, core = row // 2, row % 2
    y, zh = dp // 4, dp % 4
    z = zh * 4 + zl
    x = col
    sib_row = row + 1 - 2 * core
    has_l, has_r = col > 0, col < ncol - 1
    has_u, has_d = row > 0, row < nrow - 1
    left, right = (dp, row, jnp.maximum(col - 1, 0)), (dp, row, jnp.minimum(col + 1, ncol - 1))
    up, down = (dp, jnp.maximum(row - 1, 0), col), (dp, jnp.minimum(row + 1, nrow - 1), col)
    sibling = (dp, sib_row, col)
    x_p, x_m = (dp, row, (col + 1) % 4), (dp, row, (col + 3) % 4)
    y_p, y_m = (((y + 1) % 4) * 4 + zh, row, col), (((y + 3) % 4) * 4 + zh, row, col)

    def z_peer(d):
        other = (z + d) % 16
        return other, (y * 4 + other // 4, (other % 4) * 2 + core, col)

    T = TILE
    loads = [
        pltpu.make_async_copy(cot, s.cot, s.lsem.at[0]),
        pltpu.make_async_copy(tok.at[0, :, 0:T], s.reg.at[1, T : 3 * T], s.lsem.at[1]),
        pltpu.make_async_copy(tok.at[0, :, T : 2 * T], s.reg.at[2, T : 3 * T], s.lsem.at[2]),
        pltpu.make_async_copy(w, s.w, s.lsem.at[3]),
    ]
    for c in loads:
        c.start()

    bar = pltpu.get_barrier_semaphore()

    def greet(dev, sem=bar):
        pl.semaphore_signal(sem, inc=1, device_id=dev, device_id_type=MESH)

    for dev in (x_p, x_m, y_p, y_m, sibling, z_peer(1)[1], z_peer(15)[1]):
        greet(dev)
    other_row = row - 1 + 2 * core
    has_other = (other_row >= 0) & (other_row < nrow)

    @pl.when(has_other)
    def _():
        greet((dp, jnp.clip(other_row, 0, nrow - 1), col))

    pl.semaphore_wait(bar, 7 + has_other.astype(jnp.int32))

    plan = [
        (has_l, has_r, tok.at[0, :, 0:T], s.reg.at[3, T : 3 * T], left),
        (has_r, has_l, tok.at[0, :, T : 2 * T], s.reg.at[0, T : 3 * T], right),
    ]
    for j in range(2):
        cols = slice(T * j, T * j + T)
        plan.append((has_u, has_d, tok.at[0, 0:T, cols], s.reg.at[1 + j, 3 * T : 4 * T], up))
        plan.append((has_d, has_u, tok.at[0, T : 2 * T, cols], s.reg.at[1 + j, 0:T], down))
    for side, has in ((0, has_l), (3, has_r)):
        plan.append(
            (has & has_u, has & has_d, s.reg.at[side, T : 2 * T], s.reg.at[side, 3 * T : 4 * T], up)
        )
        plan.append(
            (has & has_d, has & has_u, s.reg.at[side, 2 * T : 3 * T], s.reg.at[side, 0:T], down)
        )

    def halo(n):
        _, _, src, dst, dev = plan[n]
        return remote(src, dst, s.hs_.at[n], s.hw_.at[n], dev)

    def start(n):
        pl.when(plan[n][0])(lambda: halo(n).start())

    def arrived(n):
        pl.when(plan[n][1])(lambda: halo(n).wait_recv())

    for n in range(6):
        start(n)

    for dev in (x_p, x_m, y_p, y_m):
        greet(dev, s.seen.at[0])
    for dev in (z_peer(1)[1], z_peer(15)[1]):
        greet(dev, s.seen.at[1])

    def tile_ok(ti, tj):
        gr, gc = row * 2 + ti - 1, col * 2 + tj - 1
        return (gr >= 0) & (gr < 2 * nrow) & (gc >= 0) & (gc < 2 * ncol)

    def tile_tokens(tj, carry):
        for ti in range(4):
            piece = s.reg[tj, T * ti : T * ti + T].astype(F32).reshape(64, D)
            piece = jnp.where(tile_ok(ti, tj), piece, 0.0)
            s.xf[64 * ti : 64 * ti + 64, :] = piece
        full = s.xf[...]
        base = pl.multiple_of(tj * 256, 256)
        s.xr[pl.ds(base, 256), :] = full.astype(BF)
        turned = full.T.reshape(4, 2, 4, 24, 256).transpose(1, 2, 0, 3, 4).reshape(D, 256)
        s.xt[:, pl.ds(base, 256)] = turned.astype(BF)
        kv = dot(s.xr[pl.ds(base, 256), :], s.w[:, F : 3 * F]).astype(BF)
        s.kv[pl.ds(base, 256), :] = kv
        s.kvt[:, pl.ds(base, 256)] = kv.astype(F32).T.astype(BF)
        s.acc[pl.ds(base, 256), :] = jnp.zeros((256, KV), F32)
        return carry

    loads[0].wait()
    loads[1].wait()
    loads[2].wait()
    for j in range(2):
        c = s.cot[0, :, T * j : T * j + T, :].astype(F32).reshape(128, F)
        s.c[128 * j : 128 * j + 128, :] = c.astype(BF)
    arrived(1)
    start(6)
    start(7)
    arrived(0)
    start(8)
    start(9)
    loads[3].wait()
    for n in range(2, 6):
        arrived(n)
    lax.fori_loop(1, 3, tile_tokens, 0)
    pl.semaphore_wait(s.seen.at[1], 2)
    greet(z_peer(2)[1], s.seen.at[2])
    greet(z_peer(14)[1], s.seen.at[2])
    for j in range(2):
        own = s.xr[(1 + j) * 256 + 64 : (1 + j) * 256 + 192, :]
        s.xto[:, 128 * j : 128 * j + 128] = s.xt[:, (1 + j) * 256 + 64 : (1 + j) * 256 + 192]
        q = dot(own, s.w[:, :F]).astype(BF).astype(F32) * (HEAD**-0.5)
        s.q[128 * j : 128 * j + 128, :] = q.astype(BF)
    groups = ((0, 256), (256, 128))

    def block_mask(W):
        rows_i = lax.broadcasted_iota(jnp.int32, (W, W), 0) // HEAD
        cols_i = lax.broadcasted_iota(jnp.int32, (W, W), 1) // HEAD
        return rows_i == cols_i

    def block_diag(part, mask, nh):
        part = part.astype(F32)
        return jnp.where(mask, jnp.concatenate([part] * nh, axis=0), 0.0).astype(BF)

    def operands(t, g0, W):
        qrow = pl.multiple_of(t * 64, 64)
        mask = block_mask(W)
        q = block_diag(s.q[pl.ds(qrow, 64), g0 : g0 + W], mask, W // HEAD)
        c = block_diag(s.c[pl.ds(qrow, 64), g0 : g0 + W], mask, W // HEAD)
        return q, c, mask, qrow

    def scores(i, tj, g0, W, qbd, cbd):
        base = pl.multiple_of(tj * 256 + 64 * i, 64)
        sc = dot(s.kv[pl.ds(base, 192), g0 : g0 + W], qbd, 1, 1)
        parts = []
        for b in range(3):
            bias = jnp.where(tile_ok(i + b, tj), 0.0, BIG)
            parts.append(sc[64 * b : 64 * b + 64] + bias)
        sc = jnp.concatenate(parts, axis=0)
        return sc, dot(s.kv[pl.ds(base, 192), F + g0 : F + g0 + W], cbd, 1, 1)

    def column_sum(value):
        return jnp.sum(value, axis=0, keepdims=True)

    def first_pass(t, carry):
        i = t % 2
        for g, (g0, W) in enumerate(groups):
            qbd, cbd, _, _ = operands(t, g0, W)
            held = [scores(i, 1 + n, g0, W, qbd, cbd) for n in range(2)]
            peak = jnp.maximum(
                jnp.max(held[0][0], axis=0, keepdims=True), jnp.max(held[1][0], axis=0, keepdims=True)
            )
            total = delta = 0.0
            for n, (sc, dp_) in enumerate(held):
                e = jnp.exp(sc - peak)
                s.sc[2 * t + g, 192 * n : 192 * n + 192, :W] = e
                s.dp[2 * t + g, 192 * n : 192 * n + 192, :W] = dp_
                total = total + column_sum(e)
                delta = delta + column_sum(e * dp_)
            s.st[2 * t + g, 0:1, :W] = peak
            s.st[2 * t + g, 1:2, :W] = total
            s.st[2 * t + g, 2:3, :W] = delta
        return carry

    def second_pass(t, carry):
        j, i = t // 2, t % 2
        for g, (g0, W) in enumerate(groups):
            nh = W // HEAD
            lanes = slice(g0, g0 + W)
            vlanes = slice(F + g0, F + g0 + W)
            qbd, cbd, mask, qrow = operands(t, g0, W)
            sc, dp2 = scores(i, 3 * j, g0, W, qbd, cbd)
            peak1 = s.st[2 * t + g, 0:1, :W]
            peak = jnp.maximum(peak1, jnp.max(sc, axis=0, keepdims=True))
            down_scale = jnp.exp(peak1 - peak)
            e2 = jnp.exp(sc - peak)
            inv = 1.0 / (s.st[2 * t + g, 1:2, :W] * down_scale + column_sum(e2))
            inv1 = down_scale * inv
            delta = s.st[2 * t + g, 2:3, :W] * inv1 + column_sum(e2 * dp2) * inv
            for n, tj in enumerate((1, 2, 3 * j)):
                if n < 2:
                    p = s.sc[2 * t + g, 192 * n : 192 * n + 192, :W] * inv1
                    dp_ = s.dp[2 * t + g, 192 * n : 192 * n + 192, :W]
                else:
                    p, dp_ = e2 * inv, dp2
                pb = p.astype(BF)
                db = (p * (dp_ - delta)).astype(BF)
                base = pl.multiple_of(tj * 256 + 64 * i, 64)
                to = pl.multiple_of((tj - j) * 256 + 64 * i, 64)
                zero = pl.multiple_of((tj - j) * 256 + 192 * (1 - i), 64)
                s.pt[pl.ds(to, 192), :W] = pb
                s.ds[pl.ds(to, 192), :W] = db
                s.pt[pl.ds(zero, 64), :W] = jnp.zeros((64, W), BF)
                s.ds[pl.ds(zero, 64), :W] = jnp.zeros((64, W), BF)
                s.acc[pl.ds(base, 192), lanes] += dot(db, qbd)
                s.acc[pl.ds(base, 192), vlanes] += dot(pb, cbd)
            wide = pl.ds(pl.multiple_of(256 * j, 256), 768)

            def fold(turned):
                kept = jnp.where(mask, turned, 0.0).T
                out = kept[0:64]
                for h in range(1, nh):
                    out = out + kept[64 * h : 64 * h + 64]
                return out

            o = fold(dot(s.kvt[vlanes, wide], s.pt[:, :W]))
            s.att[pl.ds(8 * i, 8), pl.ds(8 * j, 8), lanes] = o.reshape(8, 8, W)
            dq = fold(dot(s.kvt[lanes, wide], s.ds[:, :W])) * (HEAD**-0.5)
            s.dq[pl.ds(qrow, 64), lanes] = dq.astype(BF)
        return carry

    lax.fori_loop(0, 4, first_pass, 0)
    pl.semaphore_wait(s.seen.at[2], 2)
    greet(z_peer(4)[1], s.seen.at[3])
    greet(z_peer(12)[1], s.seen.at[3])
    for n in range(6, 10):
        arrived(n)
    lax.fori_loop(0, 2, lambda t, carry: tile_tokens(3 * t, carry), 0)
    lax.fori_loop(0, 4, second_pass, 0)
    att_o[0] = s.att[...].astype(BF)

    def pack(tj, carry):
        rows = pl.ds(pl.multiple_of(tj * 256, 256), 256)
        s.dkv[rows, :] = s.acc[rows, :].astype(BF)
        return carry

    lax.fori_loop(0, 4, pack, 0)

    vert = []
    for n, tj in enumerate((0, 3, 1, 2)):
        side = has_l if tj == 0 else has_r if tj == 3 else None
        for m, (has, back, ti, dev) in enumerate(((has_u, has_d, 0, up), (has_d, has_u, 3, down))):
            at = tj * 256 + ti * 64
            cp = remote(
                s.dkv.at[at : at + 64], s.vr.at[m, tj], s.vs.at[2 * n + m], s.vw.at[2 * n + m], dev
            )
            snd, rcv = (has, back) if side is None else (has & side, back & side)
            vert.append((snd, rcv, cp))
            pl.when(snd)(cp.start)

    def grads(half):
        at = pl.ds(pl.multiple_of(half * 384, 384), 384)
        xo, xa = s.xto[at, :], s.xt[at, :]
        return xo, xa

    def grad_half(half, put):
        xo, xa = grads(half)
        put(slice(0, F), dot(xo, s.dq[...]))
        put(slice(F, 3 * F), dot(xa, s.dkv[...]))

    def put_send(lanes, value):
        s.gs[:, lanes] = value.astype(BF)

    def put_own(lanes, value):
        s.s1[:, lanes] = value

    grad_half(1 - core, put_send)
    pair = remote(s.gs, s.gr, s.ps.at[0], s.pw.at[0], sibling)
    pair.start()
    grad_half(core, put_own)
    pair.wait()
    s.s1[...] = s.s1[...] + s.gr[...].astype(F32)
    s.s1b[...] = s.s1[...].astype(BF)

    class Ring:
        def __init__(self, m, plus, minus, half_b, half_f, buf, sems, at):
            self.m, self.half_f, self.buf = m, half_f, buf
            o, p, q = (m + 2) % 4, (m + 1) % 4, (m + 3) % 4
            self.p, self.q = p, q
            ss, rs = sems

            def cp(src, dst, n, dev):
                return remote(src, dst, ss.at[at + n], rs.at[at + n], dev)

            self.first = [
                cp(half_b(o, 0), buf.at[0], 0, plus),
                cp(half_b(o, 1), buf.at[1], 1, minus),
                cp(half_b(p, 1), buf.at[3], 2, plus),
                cp(half_b(q, 0), buf.at[4], 3, minus),
            ]
            self.second = [
                cp(buf.at[6], buf.at[2], 4, plus),
                cp(buf.at[7], buf.at[5], 5, minus),
            ]

        def start(self):
            for c in self.first:
                c.start()

        def relay(self):
            buf = self.buf
            self.first[0].wait_recv()
            buf[6] = (self.half_f(self.p, 0) + buf[0].astype(F32)).astype(BF)
            self.second[0].start()
            self.first[1].wait_recv()
            buf[7] = (self.half_f(self.q, 1) + buf[1].astype(F32)).astype(BF)
            self.second[1].start()

        def finish(self):
            buf, m = self.buf, self.m
            self.first[2].wait_recv()
            self.first[3].wait_recv()
            self.second[0].wait_recv()
            self.second[1].wait_recv()
            lo = self.half_f(m, 0) + buf[2].astype(F32) + buf[4].astype(F32)
            hi = self.half_f(m, 1) + buf[3].astype(F32) + buf[5].astype(F32)
            return lo, hi

        def sent(self):
            for c in self.first + self.second:
                c.wait_send()

    def al(v, n):
        return pl.multiple_of(v, n)

    def window(k):
        return pl.ds(al(k * 256, 256), 384)

    ax = Ring(
        x, x_p, x_m,
        lambda k, h: s.s1b.at[pl.ds(al(k * 96 + 48 * h, 48), 48), :],
        lambda k, h: s.s1[pl.ds(al(k * 96 + 48 * h, 48), 48), :],
        s.bx, (s.as_, s.aw), 0,
    )
    ay = Ring(
        y, y_p, y_m,
        lambda k, h: s.s1b.at[192 * h : 192 * h + 192, window(k)],
        lambda k, h: s.s1[192 * h : 192 * h + 192, window(k)],
        s.by, (s.as_, s.aw), 6,
    )

    @pl.when(core == 0)
    def _():
        ax.start()

    @pl.when(core == 1)
    def _():
        ay.start()

    @pl.when(core == 0)
    def _():
        ax.relay()

    @pl.when(core == 1)
    def _():
        ay.relay()

    for n in range(4):
        snd, rcv, cp = vert[n]
        pl.when(rcv)(cp.wait_recv)
    horiz = []
    for m, (has, back, tj, dev) in enumerate(((has_l, has_r, 0, left), (has_r, has_l, 3, right))):
        base = tj * 256 + 64
        cp = remote(s.hs.at[m], s.hr.at[m], s.hsem.at[m], s.hw.at[m], dev)
        horiz.append((has, back, cp))

        @pl.when(has)
        def _(m=m, base=base, tj=tj, cp=cp):
            upper = s.acc[base : base + 64, :]
            lower = s.acc[base + 64 : base + 128, :]
            upper = upper + jnp.where(has_u, s.vr[1, tj].astype(F32), 0.0)
            lower = lower + jnp.where(has_d, s.vr[0, tj].astype(F32), 0.0)
            s.hs[m, 0:64] = upper.astype(BF)
            s.hs[m, 64:128] = lower.astype(BF)
            cp.start()

    @pl.when(core == 0)
    def _():
        lo, hi = ax.finish()
        s.s2x[0:48] = lo
        s.s2x[48:96] = hi
        s.s2xb[0:48] = lo.astype(BF)
        s.s2xb[48:96] = hi.astype(BF)

    @pl.when(core == 1)
    def _():
        lo, hi = ay.finish()
        s.s2y[0:192] = lo
        s.s2y[192:384] = hi
        s.s2yb[0:192] = lo.astype(BF)
        s.s2yb[192:384] = hi.astype(BF)

    def spread(m, src, dev_of):
        copies = []
        for d in (2, 1, 3):
            k = (m + d) % 4
            cp = remote(src(k), s.b2.at[d - 1], s.bs.at[d - 1], s.bw.at[d - 1], dev_of(k))
            cp.start()
            copies.append(cp)
        return copies

    pl.semaphore_wait(s.seen.at[0], 4)

    def by():
        return spread(
            y,
            lambda k: s.s2xb.at[:, window(k)],
            lambda k: (k * 4 + zh, row, col),
        )

    def bx():
        return spread(x, lambda k: s.s2yb.at[pl.ds(al(k * 96, 96), 96), :], lambda k: (dp, row, k))

    def second(copies, own):
        for cp in copies:
            cp.wait()
        s.s3[...] = own + s.b2[0].astype(F32) + s.b2[1].astype(F32) + s.b2[2].astype(F32)

    @pl.when(core == 0)
    def _():
        second(by(), s.s2x[:, window(y)])

    @pl.when(core == 1)
    def _():
        second(bx(), s.s2y[pl.ds(al(x * 96, 96), 96), :])

    pl.semaphore_wait(s.seen.at[3], 2)

    s3 = s.s3[...]
    for k in range(1, 4):
        s3 = jnp.where(y == k, pltpu.roll(s.s3[...], 384 - 32 * k, 1), s3)
    for h in range(4):
        lanes = (s3 if h == 0 else pltpu.roll(s3, 384 - 72 * h, 1))[:, :128]
        for l in range(4):
            s.zs[4 * h + l] = lanes[24 * l : 24 * l + 24].astype(BF)
    zcopies = {}
    for d in (8, 7, 9, 6, 10, 5, 11, 4, 12, 3, 13, 2, 14, 1, 15):
        other, dev = z_peer(d)
        zcopies[d] = remote(s.zs.at[other], s.zr.at[d - 1], s.zsem.at[d - 1], s.zw.at[d - 1], dev)
        zcopies[d].start()

    for n in range(4, 8):
        snd, rcv, cp = vert[n]
        pl.when(rcv)(cp.wait_recv)
    for has, back, cp in horiz:
        pl.when(back)(cp.wait_recv)
    for j in range(2):
        base = (1 + j) * 256 + 64
        own = s.acc[base : base + 128, :]
        upper = own[0:64] + jnp.where(has_u, s.vr[1, 1 + j].astype(F32), 0.0)
        lower = own[64:128] + jnp.where(has_d, s.vr[0, 1 + j].astype(F32), 0.0)
        own = jnp.concatenate([upper, lower], axis=0)
        has, m = (has_l, 1) if j == 0 else (has_r, 0)
        own = own + jnp.where(has, s.hr[m].astype(F32), 0.0)
        gx = dot(s.dq[128 * j : 128 * j + 128, :], s.w[:, :F], 1, 1)
        gx = gx + dot(own.astype(BF), s.w[:, F:], 1, 1)
        s.gx[:, T * j : T * j + T, :] = gx.reshape(SIDE, T, D)
    gx_o[0] = s.gx[...].astype(BF)

    total = s.zs[z].astype(F32)
    for d in range(1, 16):
        zcopies[d].wait_recv()
        total = total + s.zr[d - 1].astype(F32)
    gw_o[...] = total[:, :72] * (1.0 / ndp)

    for n in range(10):
        pl.when(plan[n][0])(lambda n=n: halo(n).wait_send())
    for snd, rcv, cp in vert:
        pl.when(snd)(cp.wait_send)
    for has, back, cp in horiz:
        pl.when(has)(cp.wait_send)

    @pl.when(core == 0)
    def _():
        ax.sent()

    @pl.when(core == 1)
    def _():
        ay.sent()

    for d in range(1, 16):
        zcopies[d].wait_send()


class Scratch:
    pass


V = pltpu.VMEM
DMA = pltpu.SemaphoreType.DMA
SCRATCH = dict(
    reg=V((4, 32, 8, D), BF),
    w=V((D, 3 * F), BF),
    cot=V((1, SIDE, SIDE, F), BF),
    xf=V((256, D), F32),
    xr=V((1024, D), BF),
    xt=V((D, 1024), BF),
    xto=V((D, 256), BF),
    kv=V((1024, KV), BF),
    kvt=V((KV, 1024), BF),
    q=V((256, F), BF),
    c=V((256, F), BF),
    acc=V((1024, KV), F32),
    dq=V((256, F), BF),
    att=V((SIDE, SIDE, F), F32),
    sc=V((8, 384, 256), F32),
    dp=V((8, 384, 256), F32),
    st=V((8, 8, 256), F32),
    pt=V((768, 256), BF),
    ds=V((768, 256), BF),
    dkv=V((1024, KV), BF),
    gx=V((SIDE, SIDE, D), F32),
    gs=V((384, 1152), BF),
    gr=V((384, 1152), BF),
    s1=V((384, 1152), F32),
    s1b=V((384, 1152), BF),
    bx=V((8, 48, 1152), BF),
    by=V((8, 192, 384), BF),
    s2x=V((96, 1152), F32),
    s2xb=V((96, 1152), BF),
    s2y=V((384, 384), F32),
    s2yb=V((384, 384), BF),
    b2=V((3, 96, 384), BF),
    s3=V((96, 384), F32),
    zs=V((16, 24, 128), BF),
    zr=V((15, 24, 128), BF),
    vr=V((2, 4, 64, KV), BF),
    hs=V((2, 128, KV), BF),
    hr=V((2, 128, KV), BF),
    lsem=DMA((4,)),
    hs_=DMA((10,)),
    hw_=DMA((10,)),
    seen=pltpu.SemaphoreType.REGULAR((4,)),
    vs=DMA((8,)),
    vw=DMA((8,)),
    ps=DMA((1,)),
    pw=DMA((1,)),
    as_=DMA((12,)),
    aw=DMA((12,)),
    bs=DMA((3,)),
    bw=DMA((3,)),
    hsem=DMA((2,)),
    hw=DMA((2,)),
    zsem=DMA((15,)),
    zw=DMA((15,)),
)


def main_entry(nrow, ncol, ndp, *refs):
    s = Scratch()
    for name, ref in zip(SCRATCH, refs[6:]):
        setattr(s, name, ref)
    main_kernel(nrow, ncol, ndp, *refs[:6], s)


def body(nrow, ncol, ndp, tokens, w_qkv, grad_out):
    anywhere = pl.BlockSpec(memory_space=pl.ANY)
    vmem = pl.BlockSpec(memory_space=pltpu.VMEM)
    outs = (
        jax.ShapeDtypeStruct((1, SIDE, SIDE, F), BF),
        jax.ShapeDtypeStruct((1, SIDE, SIDE, D), BF),
        jax.ShapeDtypeStruct((24, 72), F32),
    )
    held = pl.pallas_call(
        functools.partial(main_entry, nrow, ncol, ndp),
        out_shape=outs,
        in_specs=[anywhere] * 3,
        out_specs=(vmem, vmem, vmem),
        scratch_shapes=list(SCRATCH.values()),
        compiler_params=pltpu.CompilerParams(
            collective_id=1, has_side_effects=True, vmem_limit_bytes=VLIM
        ),
        name="block",
    )(tokens, w_qkv, grad_out)
    return pl.pallas_call(
        hand_on,
        out_shape=outs,
        in_specs=[vmem] * 3,
        out_specs=(vmem, vmem, vmem),
        name="results",
    )(*held)


def hand_on(a, b, c, a_o, b_o, c_o):
    a_o[...] = a[...]
    b_o[...] = b[...]
    c_o[...] = c[...]


def solution(mesh):
    split = P("dp", "row", "col", None)
    sizes = mesh.shape
    return jax.shard_map(
        functools.partial(body, sizes["row"], sizes["col"], sizes["dp"]),
        mesh=mesh,
        in_specs=(split, P(), split),
        out_specs=(split, split, P(("row", "col"), "dp")),
        check_vma=False,
    )
```

```python
import functools

import jax
import jax.numpy as jnp
from jax import lax
from jax.experimental import pallas as pl
from jax.experimental.pallas import tpu as pltpu
from jax.sharding import PartitionSpec as P

D = 768
HEADS = 6
HEAD = 64
TILE = 8
F = HEADS * HEAD
KV = 2 * F
SIDE = 16
BF = jnp.bfloat16
F32 = jnp.float32
MESH = pl.DeviceIdType.MESH
BIG = -1e30
VLIM = 60 * 1024 * 1024


def dot(a, b, ca=1, cb=0):
    return lax.dot_general(a, b, (((ca,), (cb,)), ((), ())), preferred_element_type=F32)


def remote(src, dst, ssem, rsem, dev):
    return pltpu.make_async_remote_copy(
        src_ref=src, dst_ref=dst, send_sem=ssem, recv_sem=rsem, device_id=dev, device_id_type=MESH
    )


def position():
    dp, row, col = lax.axis_index("dp"), lax.axis_index("row"), lax.axis_index("col")
    return dp, row, col


def main_kernel(nrow, ncol, ndp, tok, w, cot, att_o, gx_o, gw_o, s):
    dp, row, col = position()
    zl, core = row // 2, row % 2
    y, zh = dp // 4, dp % 4
    z = zh * 4 + zl
    x = col
    sib_row = row + 1 - 2 * core
    has_l, has_r = col > 0, col < ncol - 1
    has_u, has_d = row > 0, row < nrow - 1
    left, right = (dp, row, jnp.maximum(col - 1, 0)), (dp, row, jnp.minimum(col + 1, ncol - 1))
    up, down = (dp, jnp.maximum(row - 1, 0), col), (dp, jnp.minimum(row + 1, nrow - 1), col)
    sibling = (dp, sib_row, col)
    x_p, x_m = (dp, row, (col + 1) % 4), (dp, row, (col + 3) % 4)
    y_p, y_m = (((y + 1) % 4) * 4 + zh, row, col), (((y + 3) % 4) * 4 + zh, row, col)

    def z_peer(d):
        other = (z + d) % 16
        return other, (y * 4 + other // 4, (other % 4) * 2 + core, col)

    T = TILE
    loads = [
        pltpu.make_async_copy(cot, s.cot, s.lsem.at[0]),
        pltpu.make_async_copy(tok.at[0, :, 0:T], s.reg.at[1, T : 3 * T], s.lsem.at[1]),
        pltpu.make_async_copy(tok.at[0, :, T : 2 * T], s.reg.at[2, T : 3 * T], s.lsem.at[2]),
        pltpu.make_async_copy(w, s.w, s.lsem.at[3]),
    ]
    for c in loads:
        c.start()

    bar = pltpu.get_barrier_semaphore()

    def greet(dev, sem=bar):
        pl.semaphore_signal(sem, inc=1, device_id=dev, device_id_type=MESH)

    for dev in (x_p, x_m, y_p, y_m, sibling, z_peer(1)[1], z_peer(15)[1]):
        greet(dev)
    other_row = row - 1 + 2 * core
    has_other = (other_row >= 0) & (other_row < nrow)

    @pl.when(has_other)
    def _():
        greet((dp, jnp.clip(other_row, 0, nrow - 1), col))

    pl.semaphore_wait(bar, 7 + has_other.astype(jnp.int32))

    plan = [
        (has_l, has_r, tok.at[0, :, 0:T], s.reg.at[3, T : 3 * T], left),
        (has_r, has_l, tok.at[0, :, T : 2 * T], s.reg.at[0, T : 3 * T], right),
    ]
    for j in range(2):
        cols = slice(T * j, T * j + T)
        plan.append((has_u, has_d, tok.at[0, 0:T, cols], s.reg.at[1 + j, 3 * T : 4 * T], up))
        plan.append((has_d, has_u, tok.at[0, T : 2 * T, cols], s.reg.at[1 + j, 0:T], down))
    for side, has in ((0, has_l), (3, has_r)):
        plan.append(
            (has & has_u, has & has_d, s.reg.at[side, T : 2 * T], s.reg.at[side, 3 * T : 4 * T], up)
        )
        plan.append(
            (has & has_d, has & has_u, s.reg.at[side, 2 * T : 3 * T], s.reg.at[side, 0:T], down)
        )

    def halo(n):
        _, _, src, dst, dev = plan[n]
        return remote(src, dst, s.hs_.at[n], s.hw_.at[n], dev)

    def start(n):
        pl.when(plan[n][0])(lambda: halo(n).start())

    def arrived(n):
        pl.when(plan[n][1])(lambda: halo(n).wait_recv())

    for n in range(6):
        start(n)

    for dev in (x_p, x_m, y_p, y_m):
        greet(dev, s.seen.at[0])
    for dev in (z_peer(1)[1], z_peer(15)[1]):
        greet(dev, s.seen.at[1])

    def tile_ok(ti, tj):
        gr, gc = row * 2 + ti - 1, col * 2 + tj - 1
        return (gr >= 0) & (gr < 2 * nrow) & (gc >= 0) & (gc < 2 * ncol)

    def tile_tokens(tj, carry):
        for ti in range(4):
            piece = s.reg[tj, T * ti : T * ti + T].astype(F32).reshape(64, D)
            piece = jnp.where(tile_ok(ti, tj), piece, 0.0)
            s.xf[64 * ti : 64 * ti + 64, :] = piece
        full = s.xf[...]
        base = pl.multiple_of(tj * 256, 256)
        s.xr[pl.ds(base, 256), :] = full.astype(BF)
        turned = full.T.reshape(4, 2, 4, 24, 256).transpose(1, 2, 0, 3, 4).reshape(D, 256)
        s.xt[:, pl.ds(base, 256)] = turned.astype(BF)
        kv = dot(s.xr[pl.ds(base, 256), :], s.w[:, F : 3 * F]).astype(BF)
        s.kv[pl.ds(base, 256), :] = kv
        s.kvt[:, pl.ds(base, 256)] = kv.astype(F32).T.astype(BF)
        s.acc[pl.ds(base, 256), :] = jnp.zeros((256, KV), F32)
        return carry

    loads[0].wait()
    loads[1].wait()
    loads[2].wait()
    for j in range(2):
        c = s.cot[0, :, T * j : T * j + T, :].astype(F32).reshape(128, F)
        s.c[128 * j : 128 * j + 128, :] = c.astype(BF)
    arrived(1)
    start(6)
    start(7)
    arrived(0)
    start(8)
    start(9)
    loads[3].wait()
    for n in range(2, 6):
        arrived(n)
    lax.fori_loop(1, 3, tile_tokens, 0)
    pl.semaphore_wait(s.seen.at[1], 2)
    greet(z_peer(2)[1], s.seen.at[2])
    greet(z_peer(14)[1], s.seen.at[2])
    for j in range(2):
        own = s.xr[(1 + j) * 256 + 64 : (1 + j) * 256 + 192, :]
        s.xto[:, 128 * j : 128 * j + 128] = s.xt[:, (1 + j) * 256 + 64 : (1 + j) * 256 + 192]
        q = dot(own, s.w[:, :F]).astype(BF).astype(F32) * (HEAD**-0.5)
        s.q[128 * j : 128 * j + 128, :] = q.astype(BF)
    groups = ((0, 256), (256, 128))

    def block_mask(W):
        rows_i = lax.broadcasted_iota(jnp.int32, (W, W), 0) // HEAD
        cols_i = lax.broadcasted_iota(jnp.int32, (W, W), 1) // HEAD
        return rows_i == cols_i

    def block_diag(part, mask, nh):
        part = part.astype(F32)
        return jnp.where(mask, jnp.concatenate([part] * nh, axis=0), 0.0).astype(BF)

    def operands(t, g0, W):
        qrow = pl.multiple_of(t * 64, 64)
        mask = block_mask(W)
        q = block_diag(s.q[pl.ds(qrow, 64), g0 : g0 + W], mask, W // HEAD)
        c = block_diag(s.c[pl.ds(qrow, 64), g0 : g0 + W], mask, W // HEAD)
        return q, c, mask, qrow

    def scores(i, tj, g0, W, qbd, cbd):
        base = pl.multiple_of(tj * 256 + 64 * i, 64)
        sc = dot(s.kv[pl.ds(base, 192), g0 : g0 + W], qbd, 1, 1)
        parts = []
        for b in range(3):
            bias = jnp.where(tile_ok(i + b, tj), 0.0, BIG)
            parts.append(sc[64 * b : 64 * b + 64] + bias)
        sc = jnp.concatenate(parts, axis=0)
        return sc, dot(s.kv[pl.ds(base, 192), F + g0 : F + g0 + W], cbd, 1, 1)

    def column_sum(value):
        return jnp.sum(value, axis=0, keepdims=True)

    def first_pass(t, carry):
        i = t % 2
        for g, (g0, W) in enumerate(groups):
            qbd, cbd, _, _ = operands(t, g0, W)
            held = [scores(i, 1 + n, g0, W, qbd, cbd) for n in range(2)]
            peak = jnp.maximum(
                jnp.max(held[0][0], axis=0, keepdims=True), jnp.max(held[1][0], axis=0, keepdims=True)
            )
            total = delta = 0.0
            for n, (sc, dp_) in enumerate(held):
                e = jnp.exp(sc - peak)
                s.sc[2 * t + g, 192 * n : 192 * n + 192, :W] = e
                s.dp[2 * t + g, 192 * n : 192 * n + 192, :W] = dp_
                total = total + column_sum(e)
                delta = delta + column_sum(e * dp_)
            s.st[2 * t + g, 0:1, :W] = peak
            s.st[2 * t + g, 1:2, :W] = total
            s.st[2 * t + g, 2:3, :W] = delta
        return carry

    def second_pass(g, t):
        g0, W = groups[g]
        j, i = t // 2, t % 2
        nh = W // HEAD
        lanes = slice(g0, g0 + W)
        vlanes = slice(F + g0, F + g0 + W)
        qbd, cbd, mask, qrow = operands(t, g0, W)
        sc, dp2 = scores(i, 3 * j, g0, W, qbd, cbd)
        peak1 = s.st[2 * t + g, 0:1, :W]
        peak = jnp.maximum(peak1, jnp.max(sc, axis=0, keepdims=True))
        down_scale = jnp.exp(peak1 - peak)
        e2 = jnp.exp(sc - peak)
        inv = 1.0 / (s.st[2 * t + g, 1:2, :W] * down_scale + column_sum(e2))
        inv1 = down_scale * inv
        delta = s.st[2 * t + g, 2:3, :W] * inv1 + column_sum(e2 * dp2) * inv
        for n, tj in enumerate((1, 2, 3 * j)):
            if n < 2:
                p = s.sc[2 * t + g, 192 * n : 192 * n + 192, :W] * inv1
                dp_ = s.dp[2 * t + g, 192 * n : 192 * n + 192, :W]
            else:
                p, dp_ = e2 * inv, dp2
            pb = p.astype(BF)
            db = (p * (dp_ - delta)).astype(BF)
            base = pl.multiple_of(tj * 256 + 64 * i, 64)
            to = pl.multiple_of((tj - j) * 256 + 64 * i, 64)
            zero = pl.multiple_of((tj - j) * 256 + 192 * (1 - i), 64)
            s.pt[pl.ds(to, 192), :W] = pb
            s.ds[pl.ds(to, 192), :W] = db
            s.pt[pl.ds(zero, 64), :W] = jnp.zeros((64, W), BF)
            s.ds[pl.ds(zero, 64), :W] = jnp.zeros((64, W), BF)
            s.acc[pl.ds(base, 192), lanes] += dot(db, qbd)
            s.acc[pl.ds(base, 192), vlanes] += dot(pb, cbd)
        wide = pl.ds(pl.multiple_of(256 * j, 256), 768)

        def fold(turned):
            kept = jnp.where(mask, turned, 0.0).T
            out = kept[0:64]
            for h in range(1, nh):
                out = out + kept[64 * h : 64 * h + 64]
            return out

        o = fold(dot(s.kvt[vlanes, wide], s.pt[:, :W]))
        s.att[pl.ds(8 * i, 8), pl.ds(8 * j, 8), lanes] = o.reshape(8, 8, W)
        dq = fold(dot(s.kvt[lanes, wide], s.ds[:, :W])) * (HEAD**-0.5)
        s.dq[pl.ds(qrow, 64), lanes] = dq.astype(BF)

    lax.fori_loop(0, 4, first_pass, 0)
    pl.semaphore_wait(s.seen.at[2], 2)
    greet(z_peer(4)[1], s.seen.at[3])
    greet(z_peer(12)[1], s.seen.at[3])
    for n in range(6, 10):
        arrived(n)
    lax.fori_loop(0, 2, lambda t, carry: tile_tokens(3 * t, carry), 0)
    class Ring:
        def __init__(self, m, plus, minus, half_b, half_f, buf, sems, at):
            self.m, self.half_f, self.buf = m, half_f, buf
            o, p, q = (m + 2) % 4, (m + 1) % 4, (m + 3) % 4
            self.p, self.q = p, q
            ss, rs = sems

            def cp(src, dst, n, dev):
                return remote(src, dst, ss.at[at + n], rs.at[at + n], dev)

            self.first = [
                cp(half_b(o, 0), buf.at[0], 0, plus),
                cp(half_b(o, 1), buf.at[1], 1, minus),
                cp(half_b(p, 1), buf.at[3], 2, plus),
                cp(half_b(q, 0), buf.at[4], 3, minus),
            ]
            self.second = [
                cp(buf.at[6], buf.at[2], 4, plus),
                cp(buf.at[7], buf.at[5], 5, minus),
            ]

        def start(self):
            for c in self.first:
                c.start()

        def relay(self):
            buf = self.buf
            self.first[0].wait_recv()
            buf[6] = (self.half_f(self.p, 0) + buf[0].astype(F32)).astype(BF)
            self.second[0].start()
            self.first[1].wait_recv()
            buf[7] = (self.half_f(self.q, 1) + buf[1].astype(F32)).astype(BF)
            self.second[1].start()

        def finish(self):
            buf, m = self.buf, self.m
            self.first[2].wait_recv()
            self.first[3].wait_recv()
            self.second[0].wait_recv()
            self.second[1].wait_recv()
            lo = self.half_f(m, 0) + buf[2].astype(F32) + buf[4].astype(F32)
            hi = self.half_f(m, 1) + buf[3].astype(F32) + buf[5].astype(F32)
            return lo, hi

        def sent(self):
            for c in self.first + self.second:
                c.wait_send()

    def al(v, n):
        return pl.multiple_of(v, n)

    def window(g, k):
        past = (k + 2) // 3
        return pl.ds(al((k + past if g == 0 else k - past) * 128, 128), groups[g][1])

    class Part:
        def __init__(self, g):
            def of(name):
                return getattr(s, name + str(g))

            self.g, self.g0, self.W = g, *groups[g]
            gs, gr, s1, s1b = of("gs"), of("gr"), of("s1"), of("s1b")
            s2x, s2xb, s2y, s2yb, b2 = of("s2x"), of("s2xb"), of("s2y"), of("s2yb"), of("b2")
            self.gs, self.gr, self.s1, self.s1b, self.b2 = gs, gr, s1, s1b, b2
            self.s2x, self.s2xb, self.s2y, self.s2yb = s2x, s2xb, s2y, s2yb
            self.pair = remote(gs, gr, s.ps.at[g], s.pw.at[g], sibling)
            self.ax = Ring(
                x, x_p, x_m,
                lambda k, h: s1b.at[pl.ds(al(k * 96 + 48 * h, 48), 48), :],
                lambda k, h: s1[pl.ds(al(k * 96 + 48 * h, 48), 48), :],
                of("bx"), (s.as_, s.aw), 12 * g,
            )
            self.ay = Ring(
                y, y_p, y_m,
                lambda k, h: s1b.at[192 * h : 192 * h + 192, window(g, k)],
                lambda k, h: s1[192 * h : 192 * h + 192, window(g, k)],
                of("by"), (s.as_, s.aw), 12 * g + 6,
            )
            self.to_y, self.to_x = [], []
            for d in (2, 1, 3):
                n = 3 * g + d - 1
                k = (y + d) % 4
                self.to_y.append(
                    remote(
                        s2xb.at[:, window(g, k)], b2.at[d - 1], s.bs.at[n], s.bw.at[n],
                        (k * 4 + zh, row, col),
                    )
                )
                k = (x + d) % 4
                self.to_x.append(
                    remote(
                        s2yb.at[pl.ds(al(k * 96, 96), 96), :], b2.at[d - 1], s.bs.at[n], s.bw.at[n],
                        (dp, row, k),
                    )
                )

        def pack(self):
            for base in range(0, 1024, 256):
                for lane in (self.g0, F + self.g0):
                    at = (slice(base, base + 256), slice(lane, lane + self.W))
                    s.dkv[at] = s.acc[at].astype(BF)

        def half(self, which, put):
            at = pl.ds(al(which * 384, 384), 384)
            W, g0 = self.W, self.g0
            put(slice(0, W), dot(s.xto[at, :], s.dq[:, g0 : g0 + W]))
            put(slice(W, 2 * W), dot(s.xt[at, :], s.dkv[:, g0 : g0 + W]))
            put(slice(2 * W, 3 * W), dot(s.xt[at, :], s.dkv[:, F + g0 : F + g0 + W]))

        def send_pair(self):
            def put(lanes, value):
                self.gs[:, lanes] = value.astype(BF)

            self.half(1 - core, put)
            self.pair.start()

        def own(self):
            def put(lanes, value):
                self.s1[:, lanes] = value

            self.half(core, put)

        def join_pair(self):
            self.pair.wait()
            both = self.s1[...] + self.gr[...].astype(F32)
            self.s1[...] = both
            self.s1b[...] = both.astype(BF)

        def start(self):
            pl.when(core == 0)(self.ax.start)
            pl.when(core == 1)(self.ay.start)

        def relay(self):
            pl.when(core == 0)(self.ax.relay)
            pl.when(core == 1)(self.ay.relay)

        def spread(self):
            @pl.when(core == 0)
            def _():
                lo, hi = self.ax.finish()
                for at, part in ((slice(0, 48), lo), (slice(48, 96), hi)):
                    self.s2x[at] = part
                    self.s2xb[at] = part.astype(BF)
                for cp in self.to_y:
                    cp.start()

            @pl.when(core == 1)
            def _():
                lo, hi = self.ay.finish()
                for at, part in ((slice(0, 192), lo), (slice(192, 384), hi)):
                    self.s2y[at] = part
                    self.s2yb[at] = part.astype(BF)
                for cp in self.to_x:
                    cp.start()

        def gather(self):
            lanes = slice(256 * self.g, 256 * self.g + self.W)

            @pl.when(core == 0)
            def _():
                for cp in self.to_y:
                    cp.wait()
                s.s3[:, lanes] = self.s2x[:, window(self.g, y)]

            @pl.when(core == 1)
            def _():
                for cp in self.to_x:
                    cp.wait()
                s.s3[:, lanes] = self.s2y[pl.ds(al(x * 96, 96), 96), :]

            b2 = self.b2
            s.s3[:, lanes] += b2[0].astype(F32) + b2[1].astype(F32) + b2[2].astype(F32)

        def sent(self):
            pl.when(core == 0)(self.ax.sent)
            pl.when(core == 1)(self.ay.sent)

    def attend(g):
        def one(t, carry):
            second_pass(g, t)
            return carry

        lax.fori_loop(0, 4, one, 0)

    first, last = Part(0), Part(1)
    attend(0)
    first.pack()
    first.send_pair()
    first.own()
    first.join_pair()
    first.start()
    attend(1)
    last.pack()

    vert = []
    for n, tj in enumerate((0, 3, 1, 2)):
        side = has_l if tj == 0 else has_r if tj == 3 else None
        for m, (has, back, ti, dev) in enumerate(((has_u, has_d, 0, up), (has_d, has_u, 3, down))):
            at = tj * 256 + ti * 64
            cp = remote(
                s.dkv.at[at : at + 64], s.vr.at[m, tj], s.vs.at[2 * n + m], s.vw.at[2 * n + m], dev
            )
            snd, rcv = (has, back) if side is None else (has & side, back & side)
            vert.append((snd, rcv, cp))

    last.send_pair()
    first.relay()
    for snd, rcv, cp in vert:
        pl.when(snd)(cp.start)
    last.own()
    last.join_pair()
    last.start()
    att_o[0] = s.att[...].astype(BF)
    pl.semaphore_wait(s.seen.at[0], 4)
    first.spread()
    last.relay()

    for n in range(4):
        snd, rcv, cp = vert[n]
        pl.when(rcv)(cp.wait_recv)
    horiz = []
    for m, (has, back, tj, dev) in enumerate(((has_l, has_r, 0, left), (has_r, has_l, 3, right))):
        base = tj * 256 + 64
        cp = remote(s.hs.at[m], s.hr.at[m], s.hsem.at[m], s.hw.at[m], dev)
        horiz.append((has, back, cp))

        @pl.when(has)
        def _(m=m, base=base, tj=tj, cp=cp):
            upper = s.acc[base : base + 64, :]
            lower = s.acc[base + 64 : base + 128, :]
            upper = upper + jnp.where(has_u, s.vr[1, tj].astype(F32), 0.0)
            lower = lower + jnp.where(has_d, s.vr[0, tj].astype(F32), 0.0)
            s.hs[m, 0:64] = upper.astype(BF)
            s.hs[m, 64:128] = lower.astype(BF)
            cp.start()

    last.spread()
    first.gather()
    last.gather()
    pl.semaphore_wait(s.seen.at[3], 2)

    a, b, c = s.s3[:, 0:128], s.s3[:, 128:256], s.s3[:, 256:384]
    inner = (y == 1) | (y == 2)
    tiles = [jnp.where(y == 1, c, a), jnp.where(y == 1, a, jnp.where(y == 2, c, b)), jnp.where(inner, b, c)]
    whole = jnp.concatenate(tiles, axis=1)
    s3 = whole
    for k in range(1, 4):
        s3 = jnp.where(y == k, pltpu.roll(whole, 384 - 32 * k, 1), s3)
    for h in range(4):
        lanes = (s3 if h == 0 else pltpu.roll(s3, 384 - 72 * h, 1))[:, :128]
        for l in range(4):
            s.zs[4 * h + l] = lanes[24 * l : 24 * l + 24].astype(BF)
    zcopies = {}
    for d in (8, 7, 9, 6, 10, 5, 11, 4, 12, 3, 13, 2, 14, 1, 15):
        other, dev = z_peer(d)
        zcopies[d] = remote(s.zs.at[other], s.zr.at[d - 1], s.zsem.at[d - 1], s.zw.at[d - 1], dev)
        zcopies[d].start()

    for n in range(4, 8):
        snd, rcv, cp = vert[n]
        pl.when(rcv)(cp.wait_recv)
    for has, back, cp in horiz:
        pl.when(back)(cp.wait_recv)
    for j in range(2):
        base = (1 + j) * 256 + 64
        own = s.acc[base : base + 128, :]
        upper = own[0:64] + jnp.where(has_u, s.vr[1, 1 + j].astype(F32), 0.0)
        lower = own[64:128] + jnp.where(has_d, s.vr[0, 1 + j].astype(F32), 0.0)
        own = jnp.concatenate([upper, lower], axis=0)
        has, m = (has_l, 1) if j == 0 else (has_r, 0)
        own = own + jnp.where(has, s.hr[m].astype(F32), 0.0)
        gx = dot(s.dq[128 * j : 128 * j + 128, :], s.w[:, :F], 1, 1)
        gx = gx + dot(own.astype(BF), s.w[:, F:], 1, 1)
        s.gx[:, T * j : T * j + T, :] = gx.reshape(SIDE, T, D)
    gx_o[0] = s.gx[...].astype(BF)

    total = s.zs[z].astype(F32)
    for d in range(1, 16):
        zcopies[d].wait_recv()
        total = total + s.zr[d - 1].astype(F32)
    gw_o[...] = total[:, :72] * (1.0 / ndp)

    for n in range(10):
        pl.when(plan[n][0])(lambda n=n: halo(n).wait_send())
    for snd, rcv, cp in vert:
        pl.when(snd)(cp.wait_send)
    for has, back, cp in horiz:
        pl.when(has)(cp.wait_send)

    first.sent()
    last.sent()
    for d in range(1, 16):
        zcopies[d].wait_send()


class Scratch:
    pass


V = pltpu.VMEM
DMA = pltpu.SemaphoreType.DMA
SCRATCH = dict(
    reg=V((4, 32, 8, D), BF),
    w=V((D, 3 * F), BF),
    cot=V((1, SIDE, SIDE, F), BF),
    xf=V((256, D), F32),
    xr=V((1024, D), BF),
    xt=V((D, 1024), BF),
    xto=V((D, 256), BF),
    kv=V((1024, KV), BF),
    kvt=V((KV, 1024), BF),
    q=V((256, F), BF),
    c=V((256, F), BF),
    acc=V((1024, KV), F32),
    dq=V((256, F), BF),
    att=V((SIDE, SIDE, F), F32),
    sc=V((8, 384, 256), F32),
    dp=V((8, 384, 256), F32),
    st=V((8, 8, 256), F32),
    pt=V((768, 256), BF),
    ds=V((768, 256), BF),
    dkv=V((1024, KV), BF),
    gx=V((SIDE, SIDE, D), F32),
    s3=V((96, 384), F32),
    zs=V((16, 24, 128), BF),
    zr=V((15, 24, 128), BF),
    vr=V((2, 4, 64, KV), BF),
    hs=V((2, 128, KV), BF),
    hr=V((2, 128, KV), BF),
    lsem=DMA((4,)),
    hs_=DMA((10,)),
    hw_=DMA((10,)),
    seen=pltpu.SemaphoreType.REGULAR((4,)),
    vs=DMA((8,)),
    vw=DMA((8,)),
    ps=DMA((2,)),
    pw=DMA((2,)),
    as_=DMA((24,)),
    aw=DMA((24,)),
    bs=DMA((6,)),
    bw=DMA((6,)),
    hsem=DMA((2,)),
    hw=DMA((2,)),
    zsem=DMA((15,)),
    zw=DMA((15,)),
)


for g_, W_ in enumerate((256, 128)):
    SCRATCH.update(
        {
            f"gs{g_}": V((384, 3 * W_), BF),
            f"gr{g_}": V((384, 3 * W_), BF),
            f"s1{g_}": V((384, 3 * W_), F32),
            f"s1b{g_}": V((384, 3 * W_), BF),
            f"bx{g_}": V((8, 48, 3 * W_), BF),
            f"by{g_}": V((8, 192, W_), BF),
            f"s2x{g_}": V((96, 3 * W_), F32),
            f"s2xb{g_}": V((96, 3 * W_), BF),
            f"s2y{g_}": V((384, W_), F32),
            f"s2yb{g_}": V((384, W_), BF),
            f"b2{g_}": V((3, 96, W_), BF),
        }
    )


def main_entry(nrow, ncol, ndp, *refs):
    s = Scratch()
    for name, ref in zip(SCRATCH, refs[6:]):
        setattr(s, name, ref)
    main_kernel(nrow, ncol, ndp, *refs[:6], s)


def body(nrow, ncol, ndp, tokens, w_qkv, grad_out):
    anywhere = pl.BlockSpec(memory_space=pl.ANY)
    vmem = pl.BlockSpec(memory_space=pltpu.VMEM)
    outs = (
        jax.ShapeDtypeStruct((1, SIDE, SIDE, F), BF),
        jax.ShapeDtypeStruct((1, SIDE, SIDE, D), BF),
        jax.ShapeDtypeStruct((24, 72), F32),
    )
    held = pl.pallas_call(
        functools.partial(main_entry, nrow, ncol, ndp),
        out_shape=outs,
        in_specs=[anywhere] * 3,
        out_specs=(vmem, vmem, vmem),
        scratch_shapes=list(SCRATCH.values()),
        compiler_params=pltpu.CompilerParams(
            collective_id=1, has_side_effects=True, vmem_limit_bytes=VLIM
        ),
        name="block",
    )(tokens, w_qkv, grad_out)
    return pl.pallas_call(
        hand_on,
        out_shape=outs,
        in_specs=[vmem] * 3,
        out_specs=(vmem, vmem, vmem),
        name="results",
    )(*held)


def hand_on(a, b, c, a_o, b_o, c_o):
    a_o[...] = a[...]
    b_o[...] = b[...]
    c_o[...] = c[...]


def solution(mesh):
    split = P("dp", "row", "col", None)
    sizes = mesh.shape
    return jax.shard_map(
        functools.partial(body, sizes["row"], sizes["col"], sizes["dp"]),
        mesh=mesh,
        in_specs=(split, P(), split),
        out_specs=(split, split, P(("row", "col"), "dp")),
        check_vma=False,
    )
```

```python
import functools

import jax
import jax.numpy as jnp
from jax import lax
from jax.experimental import pallas as pl
from jax.experimental.pallas import tpu as pltpu
from jax.sharding import PartitionSpec as P

D = 768
HEADS = 6
HEAD = 64
TILE = 8
F = HEADS * HEAD
KV = 2 * F
SIDE = 16
BF = jnp.bfloat16
F32 = jnp.float32
MESH = pl.DeviceIdType.MESH
BIG = -1e30
VLIM = 60 * 1024 * 1024


def dot(a, b, ca=1, cb=0):
    return lax.dot_general(a, b, (((ca,), (cb,)), ((), ())), preferred_element_type=F32)


def remote(src, dst, ssem, rsem, dev):
    return pltpu.make_async_remote_copy(
        src_ref=src, dst_ref=dst, send_sem=ssem, recv_sem=rsem, device_id=dev, device_id_type=MESH
    )


def position():
    dp, row, col = lax.axis_index("dp"), lax.axis_index("row"), lax.axis_index("col")
    return dp, row, col


def main_kernel(nrow, ncol, ndp, tok, w, cot, att_o, gx_o, gw_o, s):
    dp, row, col = position()
    zl, core = row // 2, row % 2
    y, zh = dp // 4, dp % 4
    z = zh * 4 + zl
    x = col
    sib_row = row + 1 - 2 * core
    has_l, has_r = col > 0, col < ncol - 1
    has_u, has_d = row > 0, row < nrow - 1
    left, right = (dp, row, jnp.maximum(col - 1, 0)), (dp, row, jnp.minimum(col + 1, ncol - 1))
    up, down = (dp, jnp.maximum(row - 1, 0), col), (dp, jnp.minimum(row + 1, nrow - 1), col)
    sibling = (dp, sib_row, col)
    x_p, x_m = (dp, row, (col + 1) % 4), (dp, row, (col + 3) % 4)
    y_p, y_m = (((y + 1) % 4) * 4 + zh, row, col), (((y + 3) % 4) * 4 + zh, row, col)

    def z_peer(d):
        other = (z + d) % 16
        return other, (y * 4 + other // 4, (other % 4) * 2 + core, col)

    T = TILE
    loads = [
        pltpu.make_async_copy(cot, s.cot, s.lsem.at[0]),
        pltpu.make_async_copy(tok.at[0, :, 0:T], s.reg.at[1, T : 3 * T], s.lsem.at[1]),
        pltpu.make_async_copy(tok.at[0, :, T : 2 * T], s.reg.at[2, T : 3 * T], s.lsem.at[2]),
        pltpu.make_async_copy(w, s.w, s.lsem.at[3]),
    ]
    for c in loads:
        c.start()

    bar = pltpu.get_barrier_semaphore()

    def greet(dev, sem=bar):
        pl.semaphore_signal(sem, inc=1, device_id=dev, device_id_type=MESH)

    for dev in (x_p, x_m, y_p, y_m, sibling, z_peer(1)[1], z_peer(15)[1]):
        greet(dev)
    other_row = row - 1 + 2 * core
    has_other = (other_row >= 0) & (other_row < nrow)

    @pl.when(has_other)
    def _():
        greet((dp, jnp.clip(other_row, 0, nrow - 1), col))

    pl.semaphore_wait(bar, 7 + has_other.astype(jnp.int32))

    plan = [
        (has_l, has_r, tok.at[0, :, 0:T], s.reg.at[3, T : 3 * T], left),
        (has_r, has_l, tok.at[0, :, T : 2 * T], s.reg.at[0, T : 3 * T], right),
    ]
    for j in range(2):
        cols = slice(T * j, T * j + T)
        plan.append((has_u, has_d, tok.at[0, 0:T, cols], s.reg.at[1 + j, 3 * T : 4 * T], up))
        plan.append((has_d, has_u, tok.at[0, T : 2 * T, cols], s.reg.at[1 + j, 0:T], down))
    for side, has in ((0, has_l), (3, has_r)):
        plan.append(
            (has & has_u, has & has_d, s.reg.at[side, T : 2 * T], s.reg.at[side, 3 * T : 4 * T], up)
        )
        plan.append(
            (has & has_d, has & has_u, s.reg.at[side, 2 * T : 3 * T], s.reg.at[side, 0:T], down)
        )

    def halo(n):
        _, _, src, dst, dev = plan[n]
        return remote(src, dst, s.hs_.at[n], s.hw_.at[n], dev)

    def start(n):
        pl.when(plan[n][0])(lambda: halo(n).start())

    def arrived(n):
        pl.when(plan[n][1])(lambda: halo(n).wait_recv())

    for n in range(6):
        start(n)

    for dev in (x_p, x_m, y_p, y_m):
        greet(dev, s.seen.at[0])
    for dev in (z_peer(1)[1], z_peer(15)[1]):
        greet(dev, s.seen.at[1])

    def tile_ok(ti, tj):
        gr, gc = row * 2 + ti - 1, col * 2 + tj - 1
        return (gr >= 0) & (gr < 2 * nrow) & (gc >= 0) & (gc < 2 * ncol)

    def tile_tokens(tj, carry):
        for ti in range(4):
            piece = s.reg[tj, T * ti : T * ti + T].astype(F32).reshape(64, D)
            piece = jnp.where(tile_ok(ti, tj), piece, 0.0)
            s.xf[64 * ti : 64 * ti + 64, :] = piece
        full = s.xf[...]
        base = pl.multiple_of(tj * 256, 256)
        s.xr[pl.ds(base, 256), :] = full.astype(BF)
        turned = full.T.reshape(4, 2, 4, 24, 256).transpose(1, 2, 0, 3, 4).reshape(D, 256)
        s.xt[:, pl.ds(base, 256)] = turned.astype(BF)
        kv = dot(s.xr[pl.ds(base, 256), :], s.w[:, F : 3 * F]).astype(BF)
        s.kv[pl.ds(base, 256), :] = kv
        s.kvt[:, pl.ds(base, 256)] = kv.astype(F32).T.astype(BF)
        s.acc[pl.ds(base, 256), :] = jnp.zeros((256, KV), F32)
        return carry

    loads[0].wait()
    loads[1].wait()
    loads[2].wait()
    for j in range(2):
        c = s.cot[0, :, T * j : T * j + T, :].astype(F32).reshape(128, F)
        s.c[128 * j : 128 * j + 128, :] = c.astype(BF)
    arrived(1)
    start(6)
    start(7)
    arrived(0)
    start(8)
    start(9)
    loads[3].wait()
    for n in range(2, 6):
        arrived(n)
    lax.fori_loop(1, 3, tile_tokens, 0)
    pl.semaphore_wait(s.seen.at[1], 2)
    greet(z_peer(2)[1], s.seen.at[2])
    greet(z_peer(14)[1], s.seen.at[2])
    for j in range(2):
        own = s.xr[(1 + j) * 256 + 64 : (1 + j) * 256 + 192, :]
        s.xto[:, 128 * j : 128 * j + 128] = s.xt[:, (1 + j) * 256 + 64 : (1 + j) * 256 + 192]
        q = dot(own, s.w[:, :F]).astype(BF).astype(F32) * (HEAD**-0.5)
        s.q[128 * j : 128 * j + 128, :] = q.astype(BF)
    groups = ((0, 256), (256, 128))

    def block_mask(W):
        rows_i = lax.broadcasted_iota(jnp.int32, (W, W), 0) // HEAD
        cols_i = lax.broadcasted_iota(jnp.int32, (W, W), 1) // HEAD
        return rows_i == cols_i

    def block_diag(part, mask, nh):
        part = part.astype(F32)
        return jnp.where(mask, jnp.concatenate([part] * nh, axis=0), 0.0).astype(BF)

    def operands(t, g0, W):
        qrow = pl.multiple_of(t * 64, 64)
        mask = block_mask(W)
        q = block_diag(s.q[pl.ds(qrow, 64), g0 : g0 + W], mask, W // HEAD)
        c = block_diag(s.c[pl.ds(qrow, 64), g0 : g0 + W], mask, W // HEAD)
        return q, c, mask, qrow

    def scores(i, tj, g0, W, qbd, cbd):
        base = pl.multiple_of(tj * 256 + 64 * i, 64)
        sc = dot(s.kv[pl.ds(base, 192), g0 : g0 + W], qbd, 1, 1)
        parts = []
        for b in range(3):
            bias = jnp.where(tile_ok(i + b, tj), 0.0, BIG)
            parts.append(sc[64 * b : 64 * b + 64] + bias)
        sc = jnp.concatenate(parts, axis=0)
        return sc, dot(s.kv[pl.ds(base, 192), F + g0 : F + g0 + W], cbd, 1, 1)

    def column_sum(value):
        return jnp.sum(value, axis=0, keepdims=True)

    def first_pass(t, carry):
        i = t % 2
        for g, (g0, W) in enumerate(groups):
            qbd, cbd, _, _ = operands(t, g0, W)
            held = [scores(i, 1 + n, g0, W, qbd, cbd) for n in range(2)]
            peak = jnp.maximum(
                jnp.max(held[0][0], axis=0, keepdims=True), jnp.max(held[1][0], axis=0, keepdims=True)
            )
            total = delta = 0.0
            for n, (sc, dp_) in enumerate(held):
                e = jnp.exp(sc - peak)
                s.sc[2 * t + g, 192 * n : 192 * n + 192, :W] = e
                s.dp[2 * t + g, 192 * n : 192 * n + 192, :W] = dp_
                total = total + column_sum(e)
                delta = delta + column_sum(e * dp_)
            s.st[2 * t + g, 0:1, :W] = peak
            s.st[2 * t + g, 1:2, :W] = total
            s.st[2 * t + g, 2:3, :W] = delta
        return carry

    def second_pass(g, t):
        g0, W = groups[g]
        j, i = t // 2, t % 2
        nh = W // HEAD
        lanes = slice(g0, g0 + W)
        vlanes = slice(F + g0, F + g0 + W)
        qbd, cbd, mask, qrow = operands(t, g0, W)
        sc, dp2 = scores(i, 3 * j, g0, W, qbd, cbd)
        peak1 = s.st[2 * t + g, 0:1, :W]
        peak = jnp.maximum(peak1, jnp.max(sc, axis=0, keepdims=True))
        down_scale = jnp.exp(peak1 - peak)
        e2 = jnp.exp(sc - peak)
        inv = 1.0 / (s.st[2 * t + g, 1:2, :W] * down_scale + column_sum(e2))
        inv1 = down_scale * inv
        delta = s.st[2 * t + g, 2:3, :W] * inv1 + column_sum(e2 * dp2) * inv
        for n, tj in enumerate((1, 2, 3 * j)):
            if n < 2:
                p = s.sc[2 * t + g, 192 * n : 192 * n + 192, :W] * inv1
                dp_ = s.dp[2 * t + g, 192 * n : 192 * n + 192, :W]
            else:
                p, dp_ = e2 * inv, dp2
            pb = p.astype(BF)
            db = (p * (dp_ - delta)).astype(BF)
            base = pl.multiple_of(tj * 256 + 64 * i, 64)
            to = pl.multiple_of((tj - j) * 256 + 64 * i, 64)
            zero = pl.multiple_of((tj - j) * 256 + 192 * (1 - i), 64)
            s.pt[pl.ds(to, 192), :W] = pb
            s.ds[pl.ds(to, 192), :W] = db
            s.pt[pl.ds(zero, 64), :W] = jnp.zeros((64, W), BF)
            s.ds[pl.ds(zero, 64), :W] = jnp.zeros((64, W), BF)
            s.acc[pl.ds(base, 192), lanes] += dot(db, qbd)
            s.acc[pl.ds(base, 192), vlanes] += dot(pb, cbd)
        wide = pl.ds(pl.multiple_of(256 * j, 256), 768)

        def fold(turned):
            kept = jnp.where(mask, turned, 0.0).T
            out = kept[0:64]
            for h in range(1, nh):
                out = out + kept[64 * h : 64 * h + 64]
            return out

        o = fold(dot(s.kvt[vlanes, wide], s.pt[:, :W]))
        s.att[pl.ds(8 * i, 8), pl.ds(8 * j, 8), lanes] = o.reshape(8, 8, W)
        dq = fold(dot(s.kvt[lanes, wide], s.ds[:, :W])) * (HEAD**-0.5)
        s.dq[pl.ds(qrow, 64), lanes] = dq.astype(BF)

    lax.fori_loop(0, 4, first_pass, 0)
    pl.semaphore_wait(s.seen.at[2], 2)
    greet(z_peer(4)[1], s.seen.at[3])
    greet(z_peer(12)[1], s.seen.at[3])
    for n in range(6, 10):
        arrived(n)
    lax.fori_loop(0, 2, lambda t, carry: tile_tokens(3 * t, carry), 0)
    class Ring:
        def __init__(self, m, plus, minus, half_b, half_f, buf, sems, at):
            self.m, self.half_f, self.buf = m, half_f, buf
            o, p, q = (m + 2) % 4, (m + 1) % 4, (m + 3) % 4
            self.p, self.q = p, q
            ss, rs = sems

            def cp(src, dst, n, dev):
                return remote(src, dst, ss.at[at + n], rs.at[at + n], dev)

            self.first = [
                cp(half_b(o, 0), buf.at[0], 0, plus),
                cp(half_b(o, 1), buf.at[1], 1, minus),
                cp(half_b(p, 1), buf.at[3], 2, plus),
                cp(half_b(q, 0), buf.at[4], 3, minus),
            ]
            self.second = [
                cp(buf.at[6], buf.at[2], 4, plus),
                cp(buf.at[7], buf.at[5], 5, minus),
            ]

        def start(self):
            for c in self.first:
                c.start()

        def relay(self):
            buf = self.buf
            self.first[0].wait_recv()
            buf[6] = (self.half_f(self.p, 0) + buf[0].astype(F32)).astype(BF)
            self.second[0].start()
            self.first[1].wait_recv()
            buf[7] = (self.half_f(self.q, 1) + buf[1].astype(F32)).astype(BF)
            self.second[1].start()

        def finish(self):
            buf, m = self.buf, self.m
            self.first[2].wait_recv()
            self.first[3].wait_recv()
            self.second[0].wait_recv()
            self.second[1].wait_recv()
            lo = self.half_f(m, 0) + buf[2].astype(F32) + buf[4].astype(F32)
            hi = self.half_f(m, 1) + buf[3].astype(F32) + buf[5].astype(F32)
            return lo, hi

        def sent(self):
            for c in self.first + self.second:
                c.wait_send()

    def al(v, n):
        return pl.multiple_of(v, n)

    def window(g, k):
        past = (k + 2) // 3
        return pl.ds(al((k + past if g == 0 else k - past) * 128, 128), groups[g][1])

    class Part:
        def __init__(self, g):
            def of(name):
                return getattr(s, name + str(g))

            self.g, self.g0, self.W = g, *groups[g]
            gs, gr, s1, s1b = of("gs"), of("gr"), of("s1"), of("s1b")
            s2x, s2xb, s2y, s2yb, b2 = of("s2x"), of("s2xb"), of("s2y"), of("s2yb"), of("b2")
            self.gs, self.gr, self.s1, self.s1b, self.b2 = gs, gr, s1, s1b, b2
            self.s2x, self.s2xb, self.s2y, self.s2yb = s2x, s2xb, s2y, s2yb
            self.pair = remote(gs, gr, s.ps.at[g], s.pw.at[g], sibling)
            self.ax = Ring(
                x, x_p, x_m,
                lambda k, h: s1b.at[pl.ds(al(k * 96 + 48 * h, 48), 48), :],
                lambda k, h: s1[pl.ds(al(k * 96 + 48 * h, 48), 48), :],
                of("bx"), (s.as_, s.aw), 12 * g,
            )
            self.ay = Ring(
                y, y_p, y_m,
                lambda k, h: s1b.at[192 * h : 192 * h + 192, window(g, k)],
                lambda k, h: s1[192 * h : 192 * h + 192, window(g, k)],
                of("by"), (s.as_, s.aw), 12 * g + 6,
            )
            self.to_y, self.to_x = [], []
            for d in (2, 1, 3):
                n = 3 * g + d - 1
                k = (y + d) % 4
                self.to_y.append(
                    remote(
                        s2xb.at[:, window(g, k)], b2.at[d - 1], s.bs.at[n], s.bw.at[n],
                        (k * 4 + zh, row, col),
                    )
                )
                k = (x + d) % 4
                self.to_x.append(
                    remote(
                        s2yb.at[pl.ds(al(k * 96, 96), 96), :], b2.at[d - 1], s.bs.at[n], s.bw.at[n],
                        (dp, row, k),
                    )
                )

        def pack(self):
            for base in range(0, 1024, 256):
                for lane in (self.g0, F + self.g0):
                    at = (slice(base, base + 256), slice(lane, lane + self.W))
                    s.dkv[at] = s.acc[at].astype(BF)

        def half(self, which, put):
            at = pl.ds(al(which * 384, 384), 384)
            W, g0 = self.W, self.g0
            put(slice(0, W), dot(s.xto[at, :], s.dq[:, g0 : g0 + W]))
            put(slice(W, 2 * W), dot(s.xt[at, :], s.dkv[:, g0 : g0 + W]))
            put(slice(2 * W, 3 * W), dot(s.xt[at, :], s.dkv[:, F + g0 : F + g0 + W]))

        def send_pair(self):
            def put(lanes, value):
                self.gs[:, lanes] = value.astype(BF)

            self.half(1 - core, put)
            self.pair.start()

        def own(self):
            def put(lanes, value):
                self.s1[:, lanes] = value

            self.half(core, put)

        def join_pair(self):
            self.pair.wait()
            both = self.s1[...] + self.gr[...].astype(F32)
            self.s1[...] = both
            self.s1b[...] = both.astype(BF)

        def start(self):
            pl.when(core == 0)(self.ax.start)
            pl.when(core == 1)(self.ay.start)

        def relay(self):
            pl.when(core == 0)(self.ax.relay)
            pl.when(core == 1)(self.ay.relay)

        def spread(self):
            @pl.when(core == 0)
            def _():
                lo, hi = self.ax.finish()
                for at, part in ((slice(0, 48), lo), (slice(48, 96), hi)):
                    self.s2x[at] = part
                    self.s2xb[at] = part.astype(BF)
                for cp in self.to_y:
                    cp.start()

            @pl.when(core == 1)
            def _():
                lo, hi = self.ay.finish()
                for at, part in ((slice(0, 192), lo), (slice(192, 384), hi)):
                    self.s2y[at] = part
                    self.s2yb[at] = part.astype(BF)
                for cp in self.to_x:
                    cp.start()

        def gather(self):
            lanes = slice(256 * self.g, 256 * self.g + self.W)

            @pl.when(core == 0)
            def _():
                for cp in self.to_y:
                    cp.wait()
                s.s3[:, lanes] = self.s2x[:, window(self.g, y)]

            @pl.when(core == 1)
            def _():
                for cp in self.to_x:
                    cp.wait()
                s.s3[:, lanes] = self.s2y[pl.ds(al(x * 96, 96), 96), :]

            b2 = self.b2
            s.s3[:, lanes] += b2[0].astype(F32) + b2[1].astype(F32) + b2[2].astype(F32)

        def sent(self):
            pl.when(core == 0)(self.ax.sent)
            pl.when(core == 1)(self.ay.sent)

    def attend(g):
        def one(t, carry):
            second_pass(g, t)
            return carry

        lax.fori_loop(0, 4, one, 0)

    first, last = Part(0), Part(1)
    attend(0)
    first.pack()
    first.send_pair()
    first.own()
    first.join_pair()
    first.start()
    attend(1)
    last.pack()

    vert = []
    for n, tj in enumerate((0, 3, 1, 2)):
        side = has_l if tj == 0 else has_r if tj == 3 else None
        for m, (has, back, ti, dev) in enumerate(((has_u, has_d, 0, up), (has_d, has_u, 3, down))):
            at = tj * 256 + ti * 64
            cp = remote(
                s.dkv.at[at : at + 64], s.vr.at[m, tj], s.vs.at[2 * n + m], s.vw.at[2 * n + m], dev
            )
            snd, rcv = (has, back) if side is None else (has & side, back & side)
            vert.append((snd, rcv, cp))

    last.send_pair()
    first.relay()
    for snd, rcv, cp in vert[:4]:
        pl.when(snd)(cp.start)
    last.own()
    last.join_pair()
    last.start()
    for snd, rcv, cp in vert[4:]:
        pl.when(snd)(cp.start)
    att_o[0] = s.att[...].astype(BF)
    last.relay()
    pl.semaphore_wait(s.seen.at[0], 4)
    first.spread()
    last.spread()

    for n in range(4):
        snd, rcv, cp = vert[n]
        pl.when(rcv)(cp.wait_recv)
    horiz = []
    for m, (has, back, tj, dev) in enumerate(((has_l, has_r, 0, left), (has_r, has_l, 3, right))):
        base = tj * 256 + 64
        cp = remote(s.hs.at[m], s.hr.at[m], s.hsem.at[m], s.hw.at[m], dev)
        horiz.append((has, back, cp))

        @pl.when(has)
        def _(m=m, base=base, tj=tj, cp=cp):
            upper = s.acc[base : base + 64, :]
            lower = s.acc[base + 64 : base + 128, :]
            upper = upper + jnp.where(has_u, s.vr[1, tj].astype(F32), 0.0)
            lower = lower + jnp.where(has_d, s.vr[0, tj].astype(F32), 0.0)
            s.hs[m, 0:64] = upper.astype(BF)
            s.hs[m, 64:128] = lower.astype(BF)
            cp.start()

    first.gather()
    last.gather()
    pl.semaphore_wait(s.seen.at[3], 2)

    a, b, c = s.s3[:, 0:128], s.s3[:, 128:256], s.s3[:, 256:384]
    inner = (y == 1) | (y == 2)
    tiles = [jnp.where(y == 1, c, a), jnp.where(y == 1, a, jnp.where(y == 2, c, b)), jnp.where(inner, b, c)]
    whole = jnp.concatenate(tiles, axis=1)
    s3 = whole
    for k in range(1, 4):
        s3 = jnp.where(y == k, pltpu.roll(whole, 384 - 32 * k, 1), s3)
    for h in range(4):
        lanes = (s3 if h == 0 else pltpu.roll(s3, 384 - 72 * h, 1))[:, :128]
        for l in range(4):
            s.zs[4 * h + l] = lanes[24 * l : 24 * l + 24].astype(BF)
    zcopies = {}
    for d in (8, 7, 9, 6, 10, 5, 11, 4, 12, 3, 13, 2, 14, 1, 15):
        other, dev = z_peer(d)
        zcopies[d] = remote(s.zs.at[other], s.zr.at[d - 1], s.zsem.at[d - 1], s.zw.at[d - 1], dev)
        zcopies[d].start()

    for n in range(4, 8):
        snd, rcv, cp = vert[n]
        pl.when(rcv)(cp.wait_recv)
    for has, back, cp in horiz:
        pl.when(back)(cp.wait_recv)
    for j in range(2):
        base = (1 + j) * 256 + 64
        own = s.acc[base : base + 128, :]
        upper = own[0:64] + jnp.where(has_u, s.vr[1, 1 + j].astype(F32), 0.0)
        lower = own[64:128] + jnp.where(has_d, s.vr[0, 1 + j].astype(F32), 0.0)
        own = jnp.concatenate([upper, lower], axis=0)
        has, m = (has_l, 1) if j == 0 else (has_r, 0)
        own = own + jnp.where(has, s.hr[m].astype(F32), 0.0)
        gx = dot(s.dq[128 * j : 128 * j + 128, :], s.w[:, :F], 1, 1)
        gx = gx + dot(own.astype(BF), s.w[:, F:], 1, 1)
        s.gx[:, T * j : T * j + T, :] = gx.reshape(SIDE, T, D)
    gx_o[0] = s.gx[...].astype(BF)

    total = s.zs[z].astype(F32)
    for d in range(1, 16):
        zcopies[d].wait_recv()
        total = total + s.zr[d - 1].astype(F32)
    gw_o[...] = total[:, :72] * (1.0 / ndp)

    for n in range(10):
        pl.when(plan[n][0])(lambda n=n: halo(n).wait_send())
    for snd, rcv, cp in vert:
        pl.when(snd)(cp.wait_send)
    for has, back, cp in horiz:
        pl.when(has)(cp.wait_send)

    first.sent()
    last.sent()
    for d in range(1, 16):
        zcopies[d].wait_send()


class Scratch:
    pass


V = pltpu.VMEM
DMA = pltpu.SemaphoreType.DMA
SCRATCH = dict(
    reg=V((4, 32, 8, D), BF),
    w=V((D, 3 * F), BF),
    cot=V((1, SIDE, SIDE, F), BF),
    xf=V((256, D), F32),
    xr=V((1024, D), BF),
    xt=V((D, 1024), BF),
    xto=V((D, 256), BF),
    kv=V((1024, KV), BF),
    kvt=V((KV, 1024), BF),
    q=V((256, F), BF),
    c=V((256, F), BF),
    acc=V((1024, KV), F32),
    dq=V((256, F), BF),
    att=V((SIDE, SIDE, F), F32),
    sc=V((8, 384, 256), F32),
    dp=V((8, 384, 256), F32),
    st=V((8, 8, 256), F32),
    pt=V((768, 256), BF),
    ds=V((768, 256), BF),
    dkv=V((1024, KV), BF),
    gx=V((SIDE, SIDE, D), F32),
    s3=V((96, 384), F32),
    zs=V((16, 24, 128), BF),
    zr=V((15, 24, 128), BF),
    vr=V((2, 4, 64, KV), BF),
    hs=V((2, 128, KV), BF),
    hr=V((2, 128, KV), BF),
    lsem=DMA((4,)),
    hs_=DMA((10,)),
    hw_=DMA((10,)),
    seen=pltpu.SemaphoreType.REGULAR((4,)),
    vs=DMA((8,)),
    vw=DMA((8,)),
    ps=DMA((2,)),
    pw=DMA((2,)),
    as_=DMA((24,)),
    aw=DMA((24,)),
    bs=DMA((6,)),
    bw=DMA((6,)),
    hsem=DMA((2,)),
    hw=DMA((2,)),
    zsem=DMA((15,)),
    zw=DMA((15,)),
)


for g_, W_ in enumerate((256, 128)):
    SCRATCH.update(
        {
            f"gs{g_}": V((384, 3 * W_), BF),
            f"gr{g_}": V((384, 3 * W_), BF),
            f"s1{g_}": V((384, 3 * W_), F32),
            f"s1b{g_}": V((384, 3 * W_), BF),
            f"bx{g_}": V((8, 48, 3 * W_), BF),
            f"by{g_}": V((8, 192, W_), BF),
            f"s2x{g_}": V((96, 3 * W_), F32),
            f"s2xb{g_}": V((96, 3 * W_), BF),
            f"s2y{g_}": V((384, W_), F32),
            f"s2yb{g_}": V((384, W_), BF),
            f"b2{g_}": V((3, 96, W_), BF),
        }
    )


def main_entry(nrow, ncol, ndp, *refs):
    s = Scratch()
    for name, ref in zip(SCRATCH, refs[6:]):
        setattr(s, name, ref)
    main_kernel(nrow, ncol, ndp, *refs[:6], s)


def body(nrow, ncol, ndp, tokens, w_qkv, grad_out):
    anywhere = pl.BlockSpec(memory_space=pl.ANY)
    vmem = pl.BlockSpec(memory_space=pltpu.VMEM)
    outs = (
        jax.ShapeDtypeStruct((1, SIDE, SIDE, F), BF),
        jax.ShapeDtypeStruct((1, SIDE, SIDE, D), BF),
        jax.ShapeDtypeStruct((24, 72), F32),
    )
    held = pl.pallas_call(
        functools.partial(main_entry, nrow, ncol, ndp),
        out_shape=outs,
        in_specs=[anywhere] * 3,
        out_specs=(vmem, vmem, vmem),
        scratch_shapes=list(SCRATCH.values()),
        compiler_params=pltpu.CompilerParams(
            collective_id=1, has_side_effects=True, vmem_limit_bytes=VLIM
        ),
        name="block",
    )(tokens, w_qkv, grad_out)
    return pl.pallas_call(
        hand_on,
        out_shape=outs,
        in_specs=[vmem] * 3,
        out_specs=(vmem, vmem, vmem),
        name="results",
    )(*held)


def hand_on(a, b, c, a_o, b_o, c_o):
    a_o[...] = a[...]
    b_o[...] = b[...]
    c_o[...] = c[...]


def solution(mesh):
    split = P("dp", "row", "col", None)
    sizes = mesh.shape
    return jax.shard_map(
        functools.partial(body, sizes["row"], sizes["col"], sizes["dp"]),
        mesh=mesh,
        in_specs=(split, P(), split),
        out_specs=(split, split, P(("row", "col"), "dp")),
        check_vma=False,
    )
```

```python
import functools

import jax
import jax.numpy as jnp
from jax import lax
from jax.experimental import pallas as pl
from jax.experimental.pallas import tpu as pltpu
from jax.sharding import PartitionSpec as P

D = 768
HEADS = 6
HEAD = 64
TILE = 8
F = HEADS * HEAD
KV = 2 * F
SIDE = 16
BF = jnp.bfloat16
F32 = jnp.float32
MESH = pl.DeviceIdType.MESH
BIG = -1e30
VLIM = 60 * 1024 * 1024


def dot(a, b, ca=1, cb=0):
    return lax.dot_general(a, b, (((ca,), (cb,)), ((), ())), preferred_element_type=F32)


def remote(src, dst, ssem, rsem, dev):
    return pltpu.make_async_remote_copy(
        src_ref=src, dst_ref=dst, send_sem=ssem, recv_sem=rsem, device_id=dev, device_id_type=MESH
    )


def position():
    dp, row, col = lax.axis_index("dp"), lax.axis_index("row"), lax.axis_index("col")
    return dp, row, col


def main_kernel(nrow, ncol, ndp, tok, w, cot, att_o, gx_o, gw_o, s):
    dp, row, col = position()
    zl, core = row // 2, row % 2
    y, zh = dp // 4, dp % 4
    z = zh * 4 + zl
    x = col
    sib_row = row + 1 - 2 * core
    has_l, has_r = col > 0, col < ncol - 1
    has_u, has_d = row > 0, row < nrow - 1
    left, right = (dp, row, jnp.maximum(col - 1, 0)), (dp, row, jnp.minimum(col + 1, ncol - 1))
    up, down = (dp, jnp.maximum(row - 1, 0), col), (dp, jnp.minimum(row + 1, nrow - 1), col)
    sibling = (dp, sib_row, col)
    x_p, x_m = (dp, row, (col + 1) % 4), (dp, row, (col + 3) % 4)
    y_p, y_m = (((y + 1) % 4) * 4 + zh, row, col), (((y + 3) % 4) * 4 + zh, row, col)

    def z_peer(d):
        other = (z + d) % 16
        return other, (y * 4 + other // 4, (other % 4) * 2 + core, col)

    T = TILE
    loads = [
        pltpu.make_async_copy(cot, s.cot, s.lsem.at[0]),
        pltpu.make_async_copy(tok.at[0, :, 0:T], s.reg.at[1, T : 3 * T], s.lsem.at[1]),
        pltpu.make_async_copy(tok.at[0, :, T : 2 * T], s.reg.at[2, T : 3 * T], s.lsem.at[2]),
        pltpu.make_async_copy(w, s.w, s.lsem.at[3]),
    ]
    for c in loads:
        c.start()

    bar = pltpu.get_barrier_semaphore()

    def greet(dev, sem=bar):
        pl.semaphore_signal(sem, inc=1, device_id=dev, device_id_type=MESH)

    for dev in (x_p, x_m, y_p, y_m, sibling, z_peer(1)[1], z_peer(15)[1]):
        greet(dev)
    other_row = row - 1 + 2 * core
    has_other = (other_row >= 0) & (other_row < nrow)

    @pl.when(has_other)
    def _():
        greet((dp, jnp.clip(other_row, 0, nrow - 1), col))

    pl.semaphore_wait(bar, 7 + has_other.astype(jnp.int32))

    plan = [
        (has_l, has_r, tok.at[0, :, 0:T], s.reg.at[3, T : 3 * T], left),
        (has_r, has_l, tok.at[0, :, T : 2 * T], s.reg.at[0, T : 3 * T], right),
    ]
    for j in range(2):
        cols = slice(T * j, T * j + T)
        plan.append((has_u, has_d, tok.at[0, 0:T, cols], s.reg.at[1 + j, 3 * T : 4 * T], up))
        plan.append((has_d, has_u, tok.at[0, T : 2 * T, cols], s.reg.at[1 + j, 0:T], down))
    for side, has in ((0, has_l), (3, has_r)):
        plan.append(
            (has & has_u, has & has_d, s.reg.at[side, T : 2 * T], s.reg.at[side, 3 * T : 4 * T], up)
        )
        plan.append(
            (has & has_d, has & has_u, s.reg.at[side, 2 * T : 3 * T], s.reg.at[side, 0:T], down)
        )

    def halo(n):
        _, _, src, dst, dev = plan[n]
        return remote(src, dst, s.hs_.at[n], s.hw_.at[n], dev)

    def start(n):
        pl.when(plan[n][0])(lambda: halo(n).start())

    def arrived(n):
        pl.when(plan[n][1])(lambda: halo(n).wait_recv())

    for n in range(6):
        start(n)

    for dev in (x_p, x_m, y_p, y_m):
        greet(dev, s.seen.at[0])
    for dev in (z_peer(1)[1], z_peer(15)[1]):
        greet(dev, s.seen.at[1])

    def tile_ok(ti, tj):
        gr, gc = row * 2 + ti - 1, col * 2 + tj - 1
        return (gr >= 0) & (gr < 2 * nrow) & (gc >= 0) & (gc < 2 * ncol)

    def tile_tokens(tj, carry):
        for ti in range(4):
            piece = s.reg[tj, T * ti : T * ti + T].astype(F32).reshape(64, D)
            piece = jnp.where(tile_ok(ti, tj), piece, 0.0)
            s.xf[64 * ti : 64 * ti + 64, :] = piece
        full = s.xf[...]
        base = pl.multiple_of(tj * 256, 256)
        s.xr[pl.ds(base, 256), :] = full.astype(BF)
        turned = full.T.reshape(4, 2, 4, 24, 256).transpose(1, 2, 0, 3, 4).reshape(D, 256)
        s.xt[:, pl.ds(base, 256)] = turned.astype(BF)
        kv = dot(s.xr[pl.ds(base, 256), :], s.w[:, F : 3 * F]).astype(BF)
        s.kv[pl.ds(base, 256), :] = kv
        s.kvt[:, pl.ds(base, 256)] = kv.astype(F32).T.astype(BF)
        s.acc[pl.ds(base, 256), :] = jnp.zeros((256, KV), F32)
        return carry

    loads[0].wait()
    loads[1].wait()
    loads[2].wait()
    for j in range(2):
        c = s.cot[0, :, T * j : T * j + T, :].astype(F32).reshape(128, F)
        s.c[128 * j : 128 * j + 128, :] = c.astype(BF)
    arrived(1)
    start(6)
    start(7)
    arrived(0)
    start(8)
    start(9)
    loads[3].wait()
    for n in range(2, 6):
        arrived(n)
    lax.fori_loop(1, 3, tile_tokens, 0)
    pl.semaphore_wait(s.seen.at[1], 2)
    greet(z_peer(2)[1], s.seen.at[2])
    greet(z_peer(14)[1], s.seen.at[2])
    for j in range(2):
        own = s.xr[(1 + j) * 256 + 64 : (1 + j) * 256 + 192, :]
        s.xto[:, 128 * j : 128 * j + 128] = s.xt[:, (1 + j) * 256 + 64 : (1 + j) * 256 + 192]
        q = dot(own, s.w[:, :F]).astype(BF).astype(F32) * (HEAD**-0.5)
        s.q[128 * j : 128 * j + 128, :] = q.astype(BF)
    groups = ((0, 256), (256, 128))

    def block_mask(W):
        rows_i = lax.broadcasted_iota(jnp.int32, (W, W), 0) // HEAD
        cols_i = lax.broadcasted_iota(jnp.int32, (W, W), 1) // HEAD
        return rows_i == cols_i

    def block_diag(part, mask, nh):
        part = part.astype(F32)
        return jnp.where(mask, jnp.concatenate([part] * nh, axis=0), 0.0).astype(BF)

    def operands(t, g0, W):
        qrow = pl.multiple_of(t * 64, 64)
        mask = block_mask(W)
        q = block_diag(s.q[pl.ds(qrow, 64), g0 : g0 + W], mask, W // HEAD)
        c = block_diag(s.c[pl.ds(qrow, 64), g0 : g0 + W], mask, W // HEAD)
        return q, c, mask, qrow

    def scores(i, tj, g0, W, qbd, cbd):
        base = pl.multiple_of(tj * 256 + 64 * i, 64)
        sc = dot(s.kv[pl.ds(base, 192), g0 : g0 + W], qbd, 1, 1)
        parts = []
        for b in range(3):
            bias = jnp.where(tile_ok(i + b, tj), 0.0, BIG)
            parts.append(sc[64 * b : 64 * b + 64] + bias)
        sc = jnp.concatenate(parts, axis=0)
        return sc, dot(s.kv[pl.ds(base, 192), F + g0 : F + g0 + W], cbd, 1, 1)

    def column_sum(value):
        return jnp.sum(value, axis=0, keepdims=True)

    def first_pass(t, carry):
        i = t % 2
        for g, (g0, W) in enumerate(groups):
            qbd, cbd, _, _ = operands(t, g0, W)
            held = [scores(i, 1 + n, g0, W, qbd, cbd) for n in range(2)]
            peak = jnp.maximum(
                jnp.max(held[0][0], axis=0, keepdims=True), jnp.max(held[1][0], axis=0, keepdims=True)
            )
            total = delta = 0.0
            for n, (sc, dp_) in enumerate(held):
                e = jnp.exp(sc - peak)
                s.sc[2 * t + g, 192 * n : 192 * n + 192, :W] = e
                s.dp[2 * t + g, 192 * n : 192 * n + 192, :W] = dp_
                total = total + column_sum(e)
                delta = delta + column_sum(e * dp_)
            s.st[2 * t + g, 0:1, :W] = peak
            s.st[2 * t + g, 1:2, :W] = total
            s.st[2 * t + g, 2:3, :W] = delta
        return carry

    def second_pass(g, t):
        g0, W = groups[g]
        j, i = t // 2, t % 2
        par = t % 2
        nh = W // HEAD
        lanes = slice(g0, g0 + W)
        vlanes = slice(F + g0, F + g0 + W)
        qbd, cbd, mask, qrow = operands(t, g0, W)
        sc, dp2 = scores(i, 3 * j, g0, W, qbd, cbd)
        peak1 = s.st[2 * t + g, 0:1, :W]
        peak = jnp.maximum(peak1, jnp.max(sc, axis=0, keepdims=True))
        down_scale = jnp.exp(peak1 - peak)
        e2 = jnp.exp(sc - peak)
        inv = 1.0 / (s.st[2 * t + g, 1:2, :W] * down_scale + column_sum(e2))
        inv1 = down_scale * inv
        delta = s.st[2 * t + g, 2:3, :W] * inv1 + column_sum(e2 * dp2) * inv
        for n, tj in enumerate((1, 2, 3 * j)):
            if n < 2:
                p = s.sc[2 * t + g, 192 * n : 192 * n + 192, :W] * inv1
                dp_ = s.dp[2 * t + g, 192 * n : 192 * n + 192, :W]
            else:
                p, dp_ = e2 * inv, dp2
            pb = p.astype(BF)
            db = (p * (dp_ - delta)).astype(BF)
            base = pl.multiple_of(tj * 256 + 64 * i, 64)
            to = pl.multiple_of((tj - j) * 256 + 64 * i, 64)
            zero = pl.multiple_of((tj - j) * 256 + 192 * (1 - i), 64)
            s.pt[par, pl.ds(to, 192), :W] = pb
            s.ds[par, pl.ds(to, 192), :W] = db
            s.pt[par, pl.ds(zero, 64), :W] = jnp.zeros((64, W), BF)
            s.ds[par, pl.ds(zero, 64), :W] = jnp.zeros((64, W), BF)
            s.acc[pl.ds(base, 192), lanes] += dot(db, qbd)
            s.acc[pl.ds(base, 192), vlanes] += dot(pb, cbd)
        wide = pl.ds(pl.multiple_of(256 * j, 256), 768)

        def fold(turned):
            kept = jnp.where(mask, turned, 0.0).T
            out = kept[0:64]
            for h in range(1, nh):
                out = out + kept[64 * h : 64 * h + 64]
            return out

        o = fold(dot(s.kvt[vlanes, wide], s.pt[par, :, :W]))
        s.att[pl.ds(8 * i, 8), pl.ds(8 * j, 8), lanes] = o.reshape(8, 8, W)
        dq = fold(dot(s.kvt[lanes, wide], s.ds[par, :, :W])) * (HEAD**-0.5)
        s.dq[pl.ds(qrow, 64), lanes] = dq.astype(BF)

    lax.fori_loop(0, 4, first_pass, 0)
    pl.semaphore_wait(s.seen.at[2], 2)
    greet(z_peer(4)[1], s.seen.at[3])
    greet(z_peer(12)[1], s.seen.at[3])
    for n in range(6, 10):
        arrived(n)
    lax.fori_loop(0, 2, lambda t, carry: tile_tokens(3 * t, carry), 0)
    class Ring:
        def __init__(self, m, plus, minus, half_b, half_f, buf, sems, at):
            self.m, self.half_f, self.buf = m, half_f, buf
            o, p, q = (m + 2) % 4, (m + 1) % 4, (m + 3) % 4
            self.p, self.q = p, q
            ss, rs = sems

            def cp(src, dst, n, dev):
                return remote(src, dst, ss.at[at + n], rs.at[at + n], dev)

            self.first = [
                cp(half_b(o, 0), buf.at[0], 0, plus),
                cp(half_b(o, 1), buf.at[1], 1, minus),
                cp(half_b(p, 1), buf.at[3], 2, plus),
                cp(half_b(q, 0), buf.at[4], 3, minus),
            ]
            self.second = [
                cp(buf.at[6], buf.at[2], 4, plus),
                cp(buf.at[7], buf.at[5], 5, minus),
            ]

        def start(self):
            for c in self.first:
                c.start()

        def relay(self):
            buf = self.buf
            self.first[0].wait_recv()
            buf[6] = (self.half_f(self.p, 0) + buf[0].astype(F32)).astype(BF)
            self.second[0].start()
            self.first[1].wait_recv()
            buf[7] = (self.half_f(self.q, 1) + buf[1].astype(F32)).astype(BF)
            self.second[1].start()

        def finish(self):
            buf, m = self.buf, self.m
            self.first[2].wait_recv()
            self.first[3].wait_recv()
            self.second[0].wait_recv()
            self.second[1].wait_recv()
            lo = self.half_f(m, 0) + buf[2].astype(F32) + buf[4].astype(F32)
            hi = self.half_f(m, 1) + buf[3].astype(F32) + buf[5].astype(F32)
            return lo, hi

        def sent(self):
            for c in self.first + self.second:
                c.wait_send()

    def al(v, n):
        return pl.multiple_of(v, n)

    def window(g, k):
        past = (k + 2) // 3
        return pl.ds(al((k + past if g == 0 else k - past) * 128, 128), groups[g][1])

    class Part:
        def __init__(self, g):
            def of(name):
                return getattr(s, name + str(g))

            self.g, self.g0, self.W = g, *groups[g]
            gs, gr, s1, s1b = of("gs"), of("gr"), of("s1"), of("s1b")
            s2x, s2xb, s2y, s2yb, b2 = of("s2x"), of("s2xb"), of("s2y"), of("s2yb"), of("b2")
            self.gs, self.gr, self.s1, self.s1b, self.b2 = gs, gr, s1, s1b, b2
            self.s2x, self.s2xb, self.s2y, self.s2yb = s2x, s2xb, s2y, s2yb
            self.pair = remote(gs, gr, s.ps.at[g], s.pw.at[g], sibling)
            self.ax = Ring(
                x, x_p, x_m,
                lambda k, h: s1b.at[pl.ds(al(k * 96 + 48 * h, 48), 48), :],
                lambda k, h: s1[pl.ds(al(k * 96 + 48 * h, 48), 48), :],
                of("bx"), (s.as_, s.aw), 12 * g,
            )
            self.ay = Ring(
                y, y_p, y_m,
                lambda k, h: s1b.at[192 * h : 192 * h + 192, window(g, k)],
                lambda k, h: s1[192 * h : 192 * h + 192, window(g, k)],
                of("by"), (s.as_, s.aw), 12 * g + 6,
            )
            self.to_y, self.to_x = [], []
            for d in (2, 1, 3):
                n = 3 * g + d - 1
                k = (y + d) % 4
                self.to_y.append(
                    remote(
                        s2xb.at[:, window(g, k)], b2.at[d - 1], s.bs.at[n], s.bw.at[n],
                        (k * 4 + zh, row, col),
                    )
                )
                k = (x + d) % 4
                self.to_x.append(
                    remote(
                        s2yb.at[pl.ds(al(k * 96, 96), 96), :], b2.at[d - 1], s.bs.at[n], s.bw.at[n],
                        (dp, row, k),
                    )
                )

        def pack(self):
            for base in range(0, 1024, 256):
                for lane in (self.g0, F + self.g0):
                    at = (slice(base, base + 256), slice(lane, lane + self.W))
                    s.dkv[at] = s.acc[at].astype(BF)

        def half(self, which, put):
            at = pl.ds(al(which * 384, 384), 384)
            W, g0 = self.W, self.g0
            put(slice(0, W), dot(s.xto[at, :], s.dq[:, g0 : g0 + W]))
            put(slice(W, 2 * W), dot(s.xt[at, :], s.dkv[:, g0 : g0 + W]))
            put(slice(2 * W, 3 * W), dot(s.xt[at, :], s.dkv[:, F + g0 : F + g0 + W]))

        def send_pair(self):
            def put(lanes, value):
                self.gs[:, lanes] = value.astype(BF)

            self.half(1 - core, put)
            self.pair.start()

        def own(self):
            def put(lanes, value):
                self.s1[:, lanes] = value

            self.half(core, put)

        def join_pair(self):
            self.pair.wait()
            both = self.s1[...] + self.gr[...].astype(F32)
            self.s1[...] = both
            self.s1b[...] = both.astype(BF)

        def start(self):
            pl.when(core == 0)(self.ax.start)
            pl.when(core == 1)(self.ay.start)

        def relay(self):
            pl.when(core == 0)(self.ax.relay)
            pl.when(core == 1)(self.ay.relay)

        def spread(self):
            @pl.when(core == 0)
            def _():
                lo, hi = self.ax.finish()
                for at, part in ((slice(0, 48), lo), (slice(48, 96), hi)):
                    self.s2x[at] = part
                    self.s2xb[at] = part.astype(BF)
                for cp in self.to_y:
                    cp.start()

            @pl.when(core == 1)
            def _():
                lo, hi = self.ay.finish()
                for at, part in ((slice(0, 192), lo), (slice(192, 384), hi)):
                    self.s2y[at] = part
                    self.s2yb[at] = part.astype(BF)
                for cp in self.to_x:
                    cp.start()

        def gather(self):
            lanes = slice(256 * self.g, 256 * self.g + self.W)

            @pl.when(core == 0)
            def _():
                for cp in self.to_y:
                    cp.wait()
                s.s3[:, lanes] = self.s2x[:, window(self.g, y)]

            @pl.when(core == 1)
            def _():
                for cp in self.to_x:
                    cp.wait()
                s.s3[:, lanes] = self.s2y[pl.ds(al(x * 96, 96), 96), :]

            b2 = self.b2
            s.s3[:, lanes] += b2[0].astype(F32) + b2[1].astype(F32) + b2[2].astype(F32)

        def sent(self):
            pl.when(core == 0)(self.ax.sent)
            pl.when(core == 1)(self.ay.sent)

    def attend(g):
        def one(t, carry):
            second_pass(g, t)
            return carry

        lax.fori_loop(0, 4, one, 0, unroll=2)

    first, last = Part(0), Part(1)
    attend(0)
    first.pack()
    first.send_pair()
    first.own()
    first.join_pair()
    first.start()
    attend(1)
    last.pack()

    vert = []
    for n, tj in enumerate((0, 3, 1, 2)):
        side = has_l if tj == 0 else has_r if tj == 3 else None
        for m, (has, back, ti, dev) in enumerate(((has_u, has_d, 0, up), (has_d, has_u, 3, down))):
            at = tj * 256 + ti * 64
            cp = remote(
                s.dkv.at[at : at + 64], s.vr.at[m, tj], s.vs.at[2 * n + m], s.vw.at[2 * n + m], dev
            )
            snd, rcv = (has, back) if side is None else (has & side, back & side)
            vert.append((snd, rcv, cp))

    last.send_pair()
    first.relay()
    for snd, rcv, cp in vert[:4]:
        pl.when(snd)(cp.start)
    last.own()
    last.join_pair()
    last.start()
    for snd, rcv, cp in vert[4:]:
        pl.when(snd)(cp.start)
    att_o[0] = s.att[...].astype(BF)
    last.relay()
    pl.semaphore_wait(s.seen.at[0], 4)
    first.spread()
    last.spread()

    for n in range(4):
        snd, rcv, cp = vert[n]
        pl.when(rcv)(cp.wait_recv)
    horiz = []
    for m, (has, back, tj, dev) in enumerate(((has_l, has_r, 0, left), (has_r, has_l, 3, right))):
        base = tj * 256 + 64
        cp = remote(s.hs.at[m], s.hr.at[m], s.hsem.at[m], s.hw.at[m], dev)
        horiz.append((has, back, cp))

        @pl.when(has)
        def _(m=m, base=base, tj=tj, cp=cp):
            upper = s.acc[base : base + 64, :]
            lower = s.acc[base + 64 : base + 128, :]
            upper = upper + jnp.where(has_u, s.vr[1, tj].astype(F32), 0.0)
            lower = lower + jnp.where(has_d, s.vr[0, tj].astype(F32), 0.0)
            s.hs[m, 0:64] = upper.astype(BF)
            s.hs[m, 64:128] = lower.astype(BF)
            cp.start()

    first.gather()
    last.gather()
    pl.semaphore_wait(s.seen.at[3], 2)

    a, b, c = s.s3[:, 0:128], s.s3[:, 128:256], s.s3[:, 256:384]
    inner = (y == 1) | (y == 2)
    tiles = [jnp.where(y == 1, c, a), jnp.where(y == 1, a, jnp.where(y == 2, c, b)), jnp.where(inner, b, c)]
    whole = jnp.concatenate(tiles, axis=1)
    s3 = whole
    for k in range(1, 4):
        s3 = jnp.where(y == k, pltpu.roll(whole, 384 - 32 * k, 1), s3)
    for h in range(4):
        lanes = (s3 if h == 0 else pltpu.roll(s3, 384 - 72 * h, 1))[:, :128]
        for l in range(4):
            s.zs[4 * h + l] = lanes[24 * l : 24 * l + 24].astype(BF)
    zcopies = {}
    for d in (8, 7, 9, 6, 10, 5, 11, 4, 12, 3, 13, 2, 14, 1, 15):
        other, dev = z_peer(d)
        zcopies[d] = remote(s.zs.at[other], s.zr.at[d - 1], s.zsem.at[d - 1], s.zw.at[d - 1], dev)
        zcopies[d].start()

    for n in range(4, 8):
        snd, rcv, cp = vert[n]
        pl.when(rcv)(cp.wait_recv)
    for has, back, cp in horiz:
        pl.when(back)(cp.wait_recv)
    for j in range(2):
        base = (1 + j) * 256 + 64
        own = s.acc[base : base + 128, :]
        upper = own[0:64] + jnp.where(has_u, s.vr[1, 1 + j].astype(F32), 0.0)
        lower = own[64:128] + jnp.where(has_d, s.vr[0, 1 + j].astype(F32), 0.0)
        own = jnp.concatenate([upper, lower], axis=0)
        has, m = (has_l, 1) if j == 0 else (has_r, 0)
        own = own + jnp.where(has, s.hr[m].astype(F32), 0.0)
        gx = dot(s.dq[128 * j : 128 * j + 128, :], s.w[:, :F], 1, 1)
        gx = gx + dot(own.astype(BF), s.w[:, F:], 1, 1)
        s.gx[:, T * j : T * j + T, :] = gx.reshape(SIDE, T, D)
    gx_o[0] = s.gx[...].astype(BF)

    total = s.zs[z].astype(F32)
    for d in range(1, 16):
        zcopies[d].wait_recv()
        total = total + s.zr[d - 1].astype(F32)
    gw_o[...] = total[:, :72] * (1.0 / ndp)

    for n in range(10):
        pl.when(plan[n][0])(lambda n=n: halo(n).wait_send())
    for snd, rcv, cp in vert:
        pl.when(snd)(cp.wait_send)
    for has, back, cp in horiz:
        pl.when(has)(cp.wait_send)

    first.sent()
    last.sent()
    for d in range(1, 16):
        zcopies[d].wait_send()


class Scratch:
    pass


V = pltpu.VMEM
DMA = pltpu.SemaphoreType.DMA
SCRATCH = dict(
    reg=V((4, 32, 8, D), BF),
    w=V((D, 3 * F), BF),
    cot=V((1, SIDE, SIDE, F), BF),
    xf=V((256, D), F32),
    xr=V((1024, D), BF),
    xt=V((D, 1024), BF),
    xto=V((D, 256), BF),
    kv=V((1024, KV), BF),
    kvt=V((KV, 1024), BF),
    q=V((256, F), BF),
    c=V((256, F), BF),
    acc=V((1024, KV), F32),
    dq=V((256, F), BF),
    att=V((SIDE, SIDE, F), F32),
    sc=V((8, 384, 256), F32),
    dp=V((8, 384, 256), F32),
    st=V((8, 8, 256), F32),
    pt=V((2, 768, 256), BF),
    ds=V((2, 768, 256), BF),
    dkv=V((1024, KV), BF),
    gx=V((SIDE, SIDE, D), F32),
    s3=V((96, 384), F32),
    zs=V((16, 24, 128), BF),
    zr=V((15, 24, 128), BF),
    vr=V((2, 4, 64, KV), BF),
    hs=V((2, 128, KV), BF),
    hr=V((2, 128, KV), BF),
    lsem=DMA((4,)),
    hs_=DMA((10,)),
    hw_=DMA((10,)),
    seen=pltpu.SemaphoreType.REGULAR((4,)),
    vs=DMA((8,)),
    vw=DMA((8,)),
    ps=DMA((2,)),
    pw=DMA((2,)),
    as_=DMA((24,)),
    aw=DMA((24,)),
    bs=DMA((6,)),
    bw=DMA((6,)),
    hsem=DMA((2,)),
    hw=DMA((2,)),
    zsem=DMA((15,)),
    zw=DMA((15,)),
)


for g_, W_ in enumerate((256, 128)):
    SCRATCH.update(
        {
            f"gs{g_}": V((384, 3 * W_), BF),
            f"gr{g_}": V((384, 3 * W_), BF),
            f"s1{g_}": V((384, 3 * W_), F32),
            f"s1b{g_}": V((384, 3 * W_), BF),
            f"bx{g_}": V((8, 48, 3 * W_), BF),
            f"by{g_}": V((8, 192, W_), BF),
            f"s2x{g_}": V((96, 3 * W_), F32),
            f"s2xb{g_}": V((96, 3 * W_), BF),
            f"s2y{g_}": V((384, W_), F32),
            f"s2yb{g_}": V((384, W_), BF),
            f"b2{g_}": V((3, 96, W_), BF),
        }
    )


def main_entry(nrow, ncol, ndp, *refs):
    s = Scratch()
    for name, ref in zip(SCRATCH, refs[6:]):
        setattr(s, name, ref)
    main_kernel(nrow, ncol, ndp, *refs[:6], s)


def body(nrow, ncol, ndp, tokens, w_qkv, grad_out):
    anywhere = pl.BlockSpec(memory_space=pl.ANY)
    vmem = pl.BlockSpec(memory_space=pltpu.VMEM)
    outs = (
        jax.ShapeDtypeStruct((1, SIDE, SIDE, F), BF),
        jax.ShapeDtypeStruct((1, SIDE, SIDE, D), BF),
        jax.ShapeDtypeStruct((24, 72), F32),
    )
    held = pl.pallas_call(
        functools.partial(main_entry, nrow, ncol, ndp),
        out_shape=outs,
        in_specs=[anywhere] * 3,
        out_specs=(vmem, vmem, vmem),
        scratch_shapes=list(SCRATCH.values()),
        compiler_params=pltpu.CompilerParams(
            collective_id=1, has_side_effects=True, vmem_limit_bytes=VLIM
        ),
        name="block",
    )(tokens, w_qkv, grad_out)
    return pl.pallas_call(
        hand_on,
        out_shape=outs,
        in_specs=[vmem] * 3,
        out_specs=(vmem, vmem, vmem),
        name="results",
    )(*held)


def hand_on(a, b, c, a_o, b_o, c_o):
    a_o[...] = a[...]
    b_o[...] = b[...]
    c_o[...] = c[...]


def solution(mesh):
    split = P("dp", "row", "col", None)
    sizes = mesh.shape
    return jax.shard_map(
        functools.partial(body, sizes["row"], sizes["col"], sizes["dp"]),
        mesh=mesh,
        in_specs=(split, P(), split),
        out_specs=(split, split, P(("row", "col"), "dp")),
        check_vma=False,
    )
```

```python
import functools

import jax
import jax.numpy as jnp
from jax import lax
from jax.experimental import pallas as pl
from jax.experimental.pallas import tpu as pltpu
from jax.sharding import PartitionSpec as P

D = 768
HEADS = 6
HEAD = 64
TILE = 8
F = HEADS * HEAD
KV = 2 * F
SIDE = 16
BF = jnp.bfloat16
F32 = jnp.float32
MESH = pl.DeviceIdType.MESH
BIG = -1e30
VLIM = 60 * 1024 * 1024


def dot(a, b, ca=1, cb=0):
    return lax.dot_general(a, b, (((ca,), (cb,)), ((), ())), preferred_element_type=F32)


def remote(src, dst, ssem, rsem, dev):
    return pltpu.make_async_remote_copy(
        src_ref=src, dst_ref=dst, send_sem=ssem, recv_sem=rsem, device_id=dev, device_id_type=MESH
    )


def position():
    dp, row, col = lax.axis_index("dp"), lax.axis_index("row"), lax.axis_index("col")
    return dp, row, col


def main_kernel(nrow, ncol, ndp, tok, w, cot, att_o, gx_o, gw_o, s):
    dp, row, col = position()
    zl, core = row // 2, row % 2
    y, zh = dp // 4, dp % 4
    z = zh * 4 + zl
    x = col
    sib_row = row + 1 - 2 * core
    has_l, has_r = col > 0, col < ncol - 1
    has_u, has_d = row > 0, row < nrow - 1
    left, right = (dp, row, jnp.maximum(col - 1, 0)), (dp, row, jnp.minimum(col + 1, ncol - 1))
    up, down = (dp, jnp.maximum(row - 1, 0), col), (dp, jnp.minimum(row + 1, nrow - 1), col)
    sibling = (dp, sib_row, col)
    x_p, x_m = (dp, row, (col + 1) % 4), (dp, row, (col + 3) % 4)
    y_p, y_m = (((y + 1) % 4) * 4 + zh, row, col), (((y + 3) % 4) * 4 + zh, row, col)

    def z_peer(d):
        other = (z + d) % 16
        return other, (y * 4 + other // 4, (other % 4) * 2 + core, col)

    T = TILE
    loads = [
        pltpu.make_async_copy(cot, s.cot, s.lsem.at[0]),
        pltpu.make_async_copy(tok.at[0, :, 0:T], s.reg.at[1, T : 3 * T], s.lsem.at[1]),
        pltpu.make_async_copy(tok.at[0, :, T : 2 * T], s.reg.at[2, T : 3 * T], s.lsem.at[2]),
        pltpu.make_async_copy(w, s.w, s.lsem.at[3]),
    ]
    for c in loads:
        c.start()

    bar = pltpu.get_barrier_semaphore()

    def greet(dev, sem=bar):
        pl.semaphore_signal(sem, inc=1, device_id=dev, device_id_type=MESH)

    for dev in (x_p, x_m, y_p, y_m, sibling, z_peer(1)[1], z_peer(15)[1]):
        greet(dev)
    other_row = row - 1 + 2 * core
    has_other = (other_row >= 0) & (other_row < nrow)

    @pl.when(has_other)
    def _():
        greet((dp, jnp.clip(other_row, 0, nrow - 1), col))

    pl.semaphore_wait(bar, 7 + has_other.astype(jnp.int32))

    plan = [
        (has_l, has_r, tok.at[0, :, 0:T], s.reg.at[3, T : 3 * T], left),
        (has_r, has_l, tok.at[0, :, T : 2 * T], s.reg.at[0, T : 3 * T], right),
    ]
    for j in range(2):
        cols = slice(T * j, T * j + T)
        plan.append((has_u, has_d, tok.at[0, 0:T, cols], s.reg.at[1 + j, 3 * T : 4 * T], up))
        plan.append((has_d, has_u, tok.at[0, T : 2 * T, cols], s.reg.at[1 + j, 0:T], down))
    for side, has in ((0, has_l), (3, has_r)):
        plan.append(
            (has & has_u, has & has_d, s.reg.at[side, T : 2 * T], s.reg.at[side, 3 * T : 4 * T], up)
        )
        plan.append(
            (has & has_d, has & has_u, s.reg.at[side, 2 * T : 3 * T], s.reg.at[side, 0:T], down)
        )

    def halo(n):
        _, _, src, dst, dev = plan[n]
        return remote(src, dst, s.hs_.at[n], s.hw_.at[n], dev)

    def start(n):
        pl.when(plan[n][0])(lambda: halo(n).start())

    def arrived(n):
        pl.when(plan[n][1])(lambda: halo(n).wait_recv())

    for n in range(6):
        start(n)

    for dev in (x_p, x_m, y_p, y_m):
        greet(dev, s.seen.at[0])
    for dev in (z_peer(1)[1], z_peer(15)[1]):
        greet(dev, s.seen.at[1])

    def tile_ok(ti, tj):
        gr, gc = row * 2 + ti - 1, col * 2 + tj - 1
        return (gr >= 0) & (gr < 2 * nrow) & (gc >= 0) & (gc < 2 * ncol)

    def tile_tokens(tj, carry):
        for ti in range(4):
            piece = s.reg[tj, T * ti : T * ti + T].astype(F32).reshape(64, D)
            piece = jnp.where(tile_ok(ti, tj), piece, 0.0)
            s.xf[tj, 64 * ti : 64 * ti + 64, :] = piece
        full = s.xf[tj]
        base = pl.multiple_of(tj * 256, 256)
        s.xr[pl.ds(base, 256), :] = full.astype(BF)
        turned = full.T.reshape(4, 2, 4, 24, 256).transpose(1, 2, 0, 3, 4).reshape(D, 256)
        s.xt[:, pl.ds(base, 256)] = turned.astype(BF)
        kv = dot(s.xr[pl.ds(base, 256), :], s.w[:, F : 3 * F]).astype(BF)
        s.kv[pl.ds(base, 256), :] = kv
        s.kvt[:, pl.ds(base, 256)] = kv.astype(F32).T.astype(BF)
        s.acc[pl.ds(base, 256), :] = jnp.zeros((256, KV), F32)
        return carry

    loads[0].wait()
    loads[1].wait()
    loads[2].wait()
    for j in range(2):
        c = s.cot[0, :, T * j : T * j + T, :].astype(F32).reshape(128, F)
        s.c[128 * j : 128 * j + 128, :] = c.astype(BF)
    arrived(1)
    start(6)
    start(7)
    arrived(0)
    start(8)
    start(9)
    loads[3].wait()
    for n in range(2, 6):
        arrived(n)
    lax.fori_loop(1, 3, tile_tokens, 0, unroll=2)
    pl.semaphore_wait(s.seen.at[1], 2)
    greet(z_peer(2)[1], s.seen.at[2])
    greet(z_peer(14)[1], s.seen.at[2])
    for j in range(2):
        own = s.xr[(1 + j) * 256 + 64 : (1 + j) * 256 + 192, :]
        s.xto[:, 128 * j : 128 * j + 128] = s.xt[:, (1 + j) * 256 + 64 : (1 + j) * 256 + 192]
        q = dot(own, s.w[:, :F]).astype(BF).astype(F32) * (HEAD**-0.5)
        s.q[128 * j : 128 * j + 128, :] = q.astype(BF)
    groups = ((0, 256), (256, 128))

    def block_mask(W):
        rows_i = lax.broadcasted_iota(jnp.int32, (W, W), 0) // HEAD
        cols_i = lax.broadcasted_iota(jnp.int32, (W, W), 1) // HEAD
        return rows_i == cols_i

    def block_diag(part, mask, nh):
        part = part.astype(F32)
        return jnp.where(mask, jnp.concatenate([part] * nh, axis=0), 0.0).astype(BF)

    def operands(t, g0, W):
        qrow = pl.multiple_of(t * 64, 64)
        mask = block_mask(W)
        q = block_diag(s.q[pl.ds(qrow, 64), g0 : g0 + W], mask, W // HEAD)
        c = block_diag(s.c[pl.ds(qrow, 64), g0 : g0 + W], mask, W // HEAD)
        return q, c, mask, qrow

    def scores(i, tj, g0, W, qbd, cbd):
        base = pl.multiple_of(tj * 256 + 64 * i, 64)
        sc = dot(s.kv[pl.ds(base, 192), g0 : g0 + W], qbd, 1, 1)
        parts = []
        for b in range(3):
            bias = jnp.where(tile_ok(i + b, tj), 0.0, BIG)
            parts.append(sc[64 * b : 64 * b + 64] + bias)
        sc = jnp.concatenate(parts, axis=0)
        return sc, dot(s.kv[pl.ds(base, 192), F + g0 : F + g0 + W], cbd, 1, 1)

    def column_sum(value):
        return jnp.sum(value, axis=0, keepdims=True)

    def first_pass(t, carry):
        i = t % 2
        for g, (g0, W) in enumerate(groups):
            qbd, cbd, _, _ = operands(t, g0, W)
            held = [scores(i, 1 + n, g0, W, qbd, cbd) for n in range(2)]
            peak = jnp.maximum(
                jnp.max(held[0][0], axis=0, keepdims=True), jnp.max(held[1][0], axis=0, keepdims=True)
            )
            total = delta = 0.0
            for n, (sc, dp_) in enumerate(held):
                e = jnp.exp(sc - peak)
                s.sc[2 * t + g, 192 * n : 192 * n + 192, :W] = e
                s.dp[2 * t + g, 192 * n : 192 * n + 192, :W] = dp_
                total = total + column_sum(e)
                delta = delta + column_sum(e * dp_)
            s.st[2 * t + g, 0:1, :W] = peak
            s.st[2 * t + g, 1:2, :W] = total
            s.st[2 * t + g, 2:3, :W] = delta
        return carry

    def second_pass(g, t):
        g0, W = groups[g]
        j, i = t // 2, t % 2
        par = t
        nh = W // HEAD
        lanes = slice(g0, g0 + W)
        vlanes = slice(F + g0, F + g0 + W)
        qbd, cbd, mask, qrow = operands(t, g0, W)
        sc, dp2 = scores(i, 3 * j, g0, W, qbd, cbd)
        peak1 = s.st[2 * t + g, 0:1, :W]
        peak = jnp.maximum(peak1, jnp.max(sc, axis=0, keepdims=True))
        down_scale = jnp.exp(peak1 - peak)
        e2 = jnp.exp(sc - peak)
        inv = 1.0 / (s.st[2 * t + g, 1:2, :W] * down_scale + column_sum(e2))
        inv1 = down_scale * inv
        delta = s.st[2 * t + g, 2:3, :W] * inv1 + column_sum(e2 * dp2) * inv
        for n, tj in enumerate((1, 2, 3 * j)):
            if n < 2:
                p = s.sc[2 * t + g, 192 * n : 192 * n + 192, :W] * inv1
                dp_ = s.dp[2 * t + g, 192 * n : 192 * n + 192, :W]
            else:
                p, dp_ = e2 * inv, dp2
            pb = p.astype(BF)
            db = (p * (dp_ - delta)).astype(BF)
            base = pl.multiple_of(tj * 256 + 64 * i, 64)
            to = pl.multiple_of((tj - j) * 256 + 64 * i, 64)
            zero = pl.multiple_of((tj - j) * 256 + 192 * (1 - i), 64)
            s.pt[par, pl.ds(to, 192), :W] = pb
            s.ds[par, pl.ds(to, 192), :W] = db
            s.pt[par, pl.ds(zero, 64), :W] = jnp.zeros((64, W), BF)
            s.ds[par, pl.ds(zero, 64), :W] = jnp.zeros((64, W), BF)
            s.acc[pl.ds(base, 192), lanes] += dot(db, qbd)
            s.acc[pl.ds(base, 192), vlanes] += dot(pb, cbd)
        wide = pl.ds(pl.multiple_of(256 * j, 256), 768)

        def fold(turned):
            kept = jnp.where(mask, turned, 0.0).T
            out = kept[0:64]
            for h in range(1, nh):
                out = out + kept[64 * h : 64 * h + 64]
            return out

        o = fold(dot(s.kvt[vlanes, wide], s.pt[par, :, :W]))
        s.att[pl.ds(8 * i, 8), pl.ds(8 * j, 8), lanes] = o.reshape(8, 8, W)
        dq = fold(dot(s.kvt[lanes, wide], s.ds[par, :, :W])) * (HEAD**-0.5)
        s.dq[pl.ds(qrow, 64), lanes] = dq.astype(BF)

    lax.fori_loop(0, 4, first_pass, 0)
    pl.semaphore_wait(s.seen.at[2], 2)
    greet(z_peer(4)[1], s.seen.at[3])
    greet(z_peer(12)[1], s.seen.at[3])
    for n in range(6, 10):
        arrived(n)
    lax.fori_loop(0, 2, lambda t, carry: tile_tokens(3 * t, carry), 0, unroll=2)
    class Ring:
        def __init__(self, m, plus, minus, half_b, half_f, buf, sems, at):
            self.m, self.half_f, self.buf = m, half_f, buf
            o, p, q = (m + 2) % 4, (m + 1) % 4, (m + 3) % 4
            self.p, self.q = p, q
            ss, rs = sems

            def cp(src, dst, n, dev):
                return remote(src, dst, ss.at[at + n], rs.at[at + n], dev)

            self.first = [
                cp(half_b(o, 0), buf.at[0], 0, plus),
                cp(half_b(o, 1), buf.at[1], 1, minus),
                cp(half_b(p, 1), buf.at[3], 2, plus),
                cp(half_b(q, 0), buf.at[4], 3, minus),
            ]
            self.second = [
                cp(buf.at[6], buf.at[2], 4, plus),
                cp(buf.at[7], buf.at[5], 5, minus),
            ]

        def start(self):
            for c in self.first:
                c.start()

        def relay(self):
            buf = self.buf
            self.first[0].wait_recv()
            buf[6] = (self.half_f(self.p, 0) + buf[0].astype(F32)).astype(BF)
            self.second[0].start()
            self.first[1].wait_recv()
            buf[7] = (self.half_f(self.q, 1) + buf[1].astype(F32)).astype(BF)
            self.second[1].start()

        def finish(self):
            buf, m = self.buf, self.m
            self.first[2].wait_recv()
            self.first[3].wait_recv()
            self.second[0].wait_recv()
            self.second[1].wait_recv()
            lo = self.half_f(m, 0) + buf[2].astype(F32) + buf[4].astype(F32)
            hi = self.half_f(m, 1) + buf[3].astype(F32) + buf[5].astype(F32)
            return lo, hi

        def sent(self):
            for c in self.first + self.second:
                c.wait_send()

    def al(v, n):
        return pl.multiple_of(v, n)

    def window(g, k):
        past = (k + 2) // 3
        return pl.ds(al((k + past if g == 0 else k - past) * 128, 128), groups[g][1])

    class Part:
        def __init__(self, g):
            def of(name):
                return getattr(s, name + str(g))

            self.g, self.g0, self.W = g, *groups[g]
            gs, gr, s1, s1b = of("gs"), of("gr"), of("s1"), of("s1b")
            s2x, s2xb, s2y, s2yb, b2 = of("s2x"), of("s2xb"), of("s2y"), of("s2yb"), of("b2")
            self.gs, self.gr, self.s1, self.s1b, self.b2 = gs, gr, s1, s1b, b2
            self.s2x, self.s2xb, self.s2y, self.s2yb = s2x, s2xb, s2y, s2yb
            self.pair = remote(gs, gr, s.ps.at[g], s.pw.at[g], sibling)
            self.ax = Ring(
                x, x_p, x_m,
                lambda k, h: s1b.at[pl.ds(al(k * 96 + 48 * h, 48), 48), :],
                lambda k, h: s1[pl.ds(al(k * 96 + 48 * h, 48), 48), :],
                of("bx"), (s.as_, s.aw), 12 * g,
            )
            self.ay = Ring(
                y, y_p, y_m,
                lambda k, h: s1b.at[192 * h : 192 * h + 192, window(g, k)],
                lambda k, h: s1[192 * h : 192 * h + 192, window(g, k)],
                of("by"), (s.as_, s.aw), 12 * g + 6,
            )
            self.to_y, self.to_x = [], []
            for d in (2, 1, 3):
                n = 3 * g + d - 1
                k = (y + d) % 4
                self.to_y.append(
                    remote(
                        s2xb.at[:, window(g, k)], b2.at[d - 1], s.bs.at[n], s.bw.at[n],
                        (k * 4 + zh, row, col),
                    )
                )
                k = (x + d) % 4
                self.to_x.append(
                    remote(
                        s2yb.at[pl.ds(al(k * 96, 96), 96), :], b2.at[d - 1], s.bs.at[n], s.bw.at[n],
                        (dp, row, k),
                    )
                )

        def pack(self):
            for base in range(0, 1024, 256):
                for lane in (self.g0, F + self.g0):
                    at = (slice(base, base + 256), slice(lane, lane + self.W))
                    s.dkv[at] = s.acc[at].astype(BF)

        def half(self, which, put):
            at = pl.ds(al(which * 384, 384), 384)
            W, g0 = self.W, self.g0
            put(slice(0, W), dot(s.xto[at, :], s.dq[:, g0 : g0 + W]))
            put(slice(W, 2 * W), dot(s.xt[at, :], s.dkv[:, g0 : g0 + W]))
            put(slice(2 * W, 3 * W), dot(s.xt[at, :], s.dkv[:, F + g0 : F + g0 + W]))

        def send_pair(self):
            def put(lanes, value):
                self.gs[:, lanes] = value.astype(BF)

            self.half(1 - core, put)
            self.pair.start()

        def own(self):
            def put(lanes, value):
                self.s1[:, lanes] = value

            self.half(core, put)

        def join_pair(self):
            self.pair.wait()
            both = self.s1[...] + self.gr[...].astype(F32)
            self.s1[...] = both
            self.s1b[...] = both.astype(BF)

        def start(self):
            pl.when(core == 0)(self.ax.start)
            pl.when(core == 1)(self.ay.start)

        def relay(self):
            pl.when(core == 0)(self.ax.relay)
            pl.when(core == 1)(self.ay.relay)

        def spread(self):
            @pl.when(core == 0)
            def _():
                lo, hi = self.ax.finish()
                for at, part in ((slice(0, 48), lo), (slice(48, 96), hi)):
                    self.s2x[at] = part
                    self.s2xb[at] = part.astype(BF)
                for cp in self.to_y:
                    cp.start()

            @pl.when(core == 1)
            def _():
                lo, hi = self.ay.finish()
                for at, part in ((slice(0, 192), lo), (slice(192, 384), hi)):
                    self.s2y[at] = part
                    self.s2yb[at] = part.astype(BF)
                for cp in self.to_x:
                    cp.start()

        def gather(self):
            lanes = slice(256 * self.g, 256 * self.g + self.W)

            @pl.when(core == 0)
            def _():
                for cp in self.to_y:
                    cp.wait()
                s.s3[:, lanes] = self.s2x[:, window(self.g, y)]

            @pl.when(core == 1)
            def _():
                for cp in self.to_x:
                    cp.wait()
                s.s3[:, lanes] = self.s2y[pl.ds(al(x * 96, 96), 96), :]

            b2 = self.b2
            s.s3[:, lanes] += b2[0].astype(F32) + b2[1].astype(F32) + b2[2].astype(F32)

        def sent(self):
            pl.when(core == 0)(self.ax.sent)
            pl.when(core == 1)(self.ay.sent)

    def attend(g):
        def one(t, carry):
            second_pass(g, t)
            return carry

        lax.fori_loop(0, 4, one, 0, unroll=4)

    first, last = Part(0), Part(1)
    attend(0)
    first.pack()
    first.send_pair()
    first.own()
    first.join_pair()
    first.start()
    attend(1)
    last.pack()

    vert = []
    for n, tj in enumerate((0, 3, 1, 2)):
        side = has_l if tj == 0 else has_r if tj == 3 else None
        for m, (has, back, ti, dev) in enumerate(((has_u, has_d, 0, up), (has_d, has_u, 3, down))):
            at = tj * 256 + ti * 64
            cp = remote(
                s.dkv.at[at : at + 64], s.vr.at[m, tj], s.vs.at[2 * n + m], s.vw.at[2 * n + m], dev
            )
            snd, rcv = (has, back) if side is None else (has & side, back & side)
            vert.append((snd, rcv, cp))

    last.send_pair()
    first.relay()
    for snd, rcv, cp in vert[:4]:
        pl.when(snd)(cp.start)
    last.own()
    last.join_pair()
    last.start()
    for snd, rcv, cp in vert[4:]:
        pl.when(snd)(cp.start)
    att_o[0] = s.att[...].astype(BF)
    last.relay()
    pl.semaphore_wait(s.seen.at[0], 4)
    first.spread()
    last.spread()

    for n in range(4):
        snd, rcv, cp = vert[n]
        pl.when(rcv)(cp.wait_recv)
    horiz = []
    for m, (has, back, tj, dev) in enumerate(((has_l, has_r, 0, left), (has_r, has_l, 3, right))):
        base = tj * 256 + 64
        cp = remote(s.hs.at[m], s.hr.at[m], s.hsem.at[m], s.hw.at[m], dev)
        horiz.append((has, back, cp))

        @pl.when(has)
        def _(m=m, base=base, tj=tj, cp=cp):
            upper = s.acc[base : base + 64, :]
            lower = s.acc[base + 64 : base + 128, :]
            upper = upper + jnp.where(has_u, s.vr[1, tj].astype(F32), 0.0)
            lower = lower + jnp.where(has_d, s.vr[0, tj].astype(F32), 0.0)
            s.hs[m, 0:64] = upper.astype(BF)
            s.hs[m, 64:128] = lower.astype(BF)
            cp.start()

    first.gather()
    last.gather()
    pl.semaphore_wait(s.seen.at[3], 2)

    a, b, c = s.s3[:, 0:128], s.s3[:, 128:256], s.s3[:, 256:384]
    inner = (y == 1) | (y == 2)
    tiles = [jnp.where(y == 1, c, a), jnp.where(y == 1, a, jnp.where(y == 2, c, b)), jnp.where(inner, b, c)]
    whole = jnp.concatenate(tiles, axis=1)
    s3 = whole
    for k in range(1, 4):
        s3 = jnp.where(y == k, pltpu.roll(whole, 384 - 32 * k, 1), s3)
    for h in range(4):
        lanes = (s3 if h == 0 else pltpu.roll(s3, 384 - 72 * h, 1))[:, :128]
        for l in range(4):
            s.zs[4 * h + l] = lanes[24 * l : 24 * l + 24].astype(BF)
    zcopies = {}
    for d in (8, 7, 9, 6, 10, 5, 11, 4, 12, 3, 13, 2, 14, 1, 15):
        other, dev = z_peer(d)
        zcopies[d] = remote(s.zs.at[other], s.zr.at[d - 1], s.zsem.at[d - 1], s.zw.at[d - 1], dev)
        zcopies[d].start()

    for n in range(4, 8):
        snd, rcv, cp = vert[n]
        pl.when(rcv)(cp.wait_recv)
    for has, back, cp in horiz:
        pl.when(back)(cp.wait_recv)
    for j in range(2):
        base = (1 + j) * 256 + 64
        own = s.acc[base : base + 128, :]
        upper = own[0:64] + jnp.where(has_u, s.vr[1, 1 + j].astype(F32), 0.0)
        lower = own[64:128] + jnp.where(has_d, s.vr[0, 1 + j].astype(F32), 0.0)
        own = jnp.concatenate([upper, lower], axis=0)
        has, m = (has_l, 1) if j == 0 else (has_r, 0)
        own = own + jnp.where(has, s.hr[m].astype(F32), 0.0)
        gx = dot(s.dq[128 * j : 128 * j + 128, :], s.w[:, :F], 1, 1)
        gx = gx + dot(own.astype(BF), s.w[:, F:], 1, 1)
        s.gx[:, T * j : T * j + T, :] = gx.reshape(SIDE, T, D)
    gx_o[0] = s.gx[...].astype(BF)

    total = s.zs[z].astype(F32)
    for d in range(1, 16):
        zcopies[d].wait_recv()
        total = total + s.zr[d - 1].astype(F32)
    gw_o[...] = total[:, :72] * (1.0 / ndp)

    for n in range(10):
        pl.when(plan[n][0])(lambda n=n: halo(n).wait_send())
    for snd, rcv, cp in vert:
        pl.when(snd)(cp.wait_send)
    for has, back, cp in horiz:
        pl.when(has)(cp.wait_send)

    first.sent()
    last.sent()
    for d in range(1, 16):
        zcopies[d].wait_send()


class Scratch:
    pass


V = pltpu.VMEM
DMA = pltpu.SemaphoreType.DMA
SCRATCH = dict(
    reg=V((4, 32, 8, D), BF),
    w=V((D, 3 * F), BF),
    cot=V((1, SIDE, SIDE, F), BF),
    xf=V((4, 256, D), F32),
    xr=V((1024, D), BF),
    xt=V((D, 1024), BF),
    xto=V((D, 256), BF),
    kv=V((1024, KV), BF),
    kvt=V((KV, 1024), BF),
    q=V((256, F), BF),
    c=V((256, F), BF),
    acc=V((1024, KV), F32),
    dq=V((256, F), BF),
    att=V((SIDE, SIDE, F), F32),
    sc=V((8, 384, 256), F32),
    dp=V((8, 384, 256), F32),
    st=V((8, 8, 256), F32),
    pt=V((4, 768, 256), BF),
    ds=V((4, 768, 256), BF),
    dkv=V((1024, KV), BF),
    gx=V((SIDE, SIDE, D), F32),
    s3=V((96, 384), F32),
    zs=V((16, 24, 128), BF),
    zr=V((15, 24, 128), BF),
    vr=V((2, 4, 64, KV), BF),
    hs=V((2, 128, KV), BF),
    hr=V((2, 128, KV), BF),
    lsem=DMA((4,)),
    hs_=DMA((10,)),
    hw_=DMA((10,)),
    seen=pltpu.SemaphoreType.REGULAR((4,)),
    vs=DMA((8,)),
    vw=DMA((8,)),
    ps=DMA((2,)),
    pw=DMA((2,)),
    as_=DMA((24,)),
    aw=DMA((24,)),
    bs=DMA((6,)),
    bw=DMA((6,)),
    hsem=DMA((2,)),
    hw=DMA((2,)),
    zsem=DMA((15,)),
    zw=DMA((15,)),
)


for g_, W_ in enumerate((256, 128)):
    SCRATCH.update(
        {
            f"gs{g_}": V((384, 3 * W_), BF),
            f"gr{g_}": V((384, 3 * W_), BF),
            f"s1{g_}": V((384, 3 * W_), F32),
            f"s1b{g_}": V((384, 3 * W_), BF),
            f"bx{g_}": V((8, 48, 3 * W_), BF),
            f"by{g_}": V((8, 192, W_), BF),
            f"s2x{g_}": V((96, 3 * W_), F32),
            f"s2xb{g_}": V((96, 3 * W_), BF),
            f"s2y{g_}": V((384, W_), F32),
            f"s2yb{g_}": V((384, W_), BF),
            f"b2{g_}": V((3, 96, W_), BF),
        }
    )


def main_entry(nrow, ncol, ndp, *refs):
    s = Scratch()
    for name, ref in zip(SCRATCH, refs[6:]):
        setattr(s, name, ref)
    main_kernel(nrow, ncol, ndp, *refs[:6], s)


def body(nrow, ncol, ndp, tokens, w_qkv, grad_out):
    anywhere = pl.BlockSpec(memory_space=pl.ANY)
    vmem = pl.BlockSpec(memory_space=pltpu.VMEM)
    outs = (
        jax.ShapeDtypeStruct((1, SIDE, SIDE, F), BF),
        jax.ShapeDtypeStruct((1, SIDE, SIDE, D), BF),
        jax.ShapeDtypeStruct((24, 72), F32),
    )
    held = pl.pallas_call(
        functools.partial(main_entry, nrow, ncol, ndp),
        out_shape=outs,
        in_specs=[anywhere] * 3,
        out_specs=(vmem, vmem, vmem),
        scratch_shapes=list(SCRATCH.values()),
        compiler_params=pltpu.CompilerParams(
            collective_id=1, has_side_effects=True, vmem_limit_bytes=VLIM
        ),
        name="block",
    )(tokens, w_qkv, grad_out)
    return pl.pallas_call(
        hand_on,
        out_shape=outs,
        in_specs=[vmem] * 3,
        out_specs=(vmem, vmem, vmem),
        name="results",
    )(*held)


def hand_on(a, b, c, a_o, b_o, c_o):
    a_o[...] = a[...]
    b_o[...] = b[...]
    c_o[...] = c[...]


def solution(mesh):
    split = P("dp", "row", "col", None)
    sizes = mesh.shape
    return jax.shard_map(
        functools.partial(body, sizes["row"], sizes["col"], sizes["dp"]),
        mesh=mesh,
        in_specs=(split, P(), split),
        out_specs=(split, split, P(("row", "col"), "dp")),
        check_vma=False,
    )
```
